32 devices in a mesh: frag: 16 (over z, y, core), band: 2 (over x).
Axes of the slice: x: 2, y: 2, z: 4, core: 2. Of those that a mesh axis runs over, the one named last changes fastest.
Arguments:
- orbitals: bfloat16 [4096, 32768], P(('frag', 'band')), parts along dimension 0, may hold values from -40 to 40
- potential: float32 [524288], P('frag'), parts along dimension 0, may hold values from 0.5 to 3
Outputs:
- margin: float32 [4096, 256], P(('frag', 'band')), parts along dimension 0
- projected: float32 [4096, 256], P(('frag', 'band')), parts along dimension 0
- residuals: bfloat16 [4096, 32768], P(('frag', 'band')), parts along dimension 0
The draws below stay inside these ranges and needn't reach their ends.
There are 16 independent parts, one for each index of `frag`. The reference program is written for one: setup_inputs(seed, part) draws one part's arguments, and reference() takes and returns one part's arrays. A program takes and returns all parts, laid end to end along the dimension named above; each array names one. Nothing has to cross between parts.
All inputs are finite; a program needn't handle non-finite values.
Results may differ from the reference program's by a relative error of at most 0.034.
Values may be sent and summed in bfloat16 or wider, within the bound.
No kernel may reach another device: no remote copies, remote signals or barrier semaphores. Data moves between devices by JAX's collectives and lax.ppermute only.
A program may use at most 192 MiB of HBM per device.

```python
import math
import jax
import jax.numpy as jnp

NSIDE = 32
BANDS = 256
GRID = 32768


def draw_orbitals(key, part):
    key_scale = jax.random.fold_in(key, 11)
    key_base = jax.random.fold_in(key, 12)
    scales = jnp.exp(jax.random.uniform(key_scale, (BANDS, 1), jnp.float32, math.log(0.5), math.log(5.0)))
    base = jnp.clip(jax.random.normal(key_base, (BANDS, GRID), jnp.float32), -6.0, 6.0)
    return (base * scales).astype(jnp.bfloat16)


def setup_inputs(seed: int = 0, part: int = 0) -> dict:
    key_list = jax.random.split(jax.random.key(seed), 3)
    part_splits = jax.random.split(jax.random.fold_in(key_list[2], part), 3)
    orbitals = draw_orbitals(jax.random.fold_in(jax.random.fold_in(key_list[2], part), 71), part)
    potential = jnp.clip(jax.random.uniform(part_splits[1], (GRID,), jnp.float32, 0.5, 3.0), 0.5, 3.0)
    return dict(orbitals=orbitals, potential=potential)


def apply_hamiltonian(orbitals, potential):
    field = orbitals.astype(jnp.float32).reshape(BANDS, NSIDE, NSIDE, NSIDE)
    beside_all = jnp.zeros_like(field)
    for axis in (1, 2, 3):
        beside_all = beside_all + jnp.roll(field, 1, axis) + jnp.roll(field, -1, axis)
    pot = potential.reshape(1, NSIDE, NSIDE, NSIDE)
    result = 0.5 * (6.0 * field - beside_all) + pot * field
    return result.reshape(BANDS, GRID).astype(jnp.bfloat16)


def reference(orbitals, potential):
    applied = apply_hamiltonian(orbitals, potential)
    margin = jnp.dot(orbitals, orbitals.T, preferred_element_type=jnp.float32)
    projected = jnp.dot(applied, orbitals.T, preferred_element_type=jnp.float32)
    coefficients = (projected / jnp.diagonal(margin)[:, None]).astype(jnp.bfloat16)
    mixed = jnp.dot(coefficients, orbitals, preferred_element_type=jnp.float32)
    residuals = (applied.astype(jnp.float32) - mixed).astype(jnp.bfloat16)
    return margin, projected, residuals
```

```python
import functools

import jax
import jax.numpy as jnp
from jax import lax
from jax.experimental import pallas as pl
from jax.experimental.pallas import tpu as pltpu
from jax.sharding import PartitionSpec as P


ROWS = 16
F32 = jnp.float32
BF16 = jnp.bfloat16
ANY = pl.ANY


def call(kernel, grid, in_specs, out_specs, out_shape, args, scratch=(), aliases={}, flops=0, limit=58):
    touched = sum(a.size * a.dtype.itemsize for a in args)
    return pl.pallas_call(
        kernel,
        out_shape=out_shape,
        grid_spec=pltpu.PrefetchScalarGridSpec(
            num_scalar_prefetch=1, grid=grid, in_specs=in_specs, out_specs=out_specs, scratch_shapes=scratch
        ),
        input_output_aliases=aliases,
        compiler_params=pltpu.CompilerParams(
            dimension_semantics=("arbitrary",), vmem_limit_bytes=limit * 2**20
        ),
        cost_estimate=pl.CostEstimate(flops=flops, bytes_accessed=touched, transcendentals=0),
    )(*args)


def near(ctr, left, right, pot, side):
    size = side * side
    z = lax.broadcasted_iota(jnp.int32, ctr.shape, 1) % side
    low = jnp.where(z == 0, pltpu.roll(ctr, size - side + 1, 1), pltpu.roll(ctr, 1, 1))
    high = jnp.where(z == side - 1, pltpu.roll(ctr, side - 1, 1), pltpu.roll(ctr, size - 1, 1))
    beside = (left + right) + (pltpu.roll(ctr, side, 1) + pltpu.roll(ctr, size - side, 1)) + (low + high)
    return (3.0 + pot) * ctr - 0.5 * beside


def rowdot(a, b):
    return lax.dot_general(a, b, (((1,), (1,)), ((), ())), preferred_element_type=F32)


def pack_body(at, src, dst):
    dst[...] = src[...]


def pack(orbitals, start, width, side):
    own, size = orbitals.shape[0], side * side
    return call(
        pack_body,
        (width,),
        [pl.BlockSpec((own, size), lambda i, at: (0, lax.rem(at[0] + i, side)))],
        pl.BlockSpec((own, size), lambda i, at: (0, i)),
        jax.ShapeDtypeStruct((own, width * size), BF16),
        (start, orbitals),
    )


def apply_body(side, at, left, ctr, right, pot, out, sums, both):
    own = ctr.shape[0]

    def some(r, _):
        rows = pl.ds(r * ROWS, ROWS)
        value = near(
            ctr[rows, :].astype(F32), left[rows, :].astype(F32), right[rows, :].astype(F32), pot[...], side
        )
        out[rows, :] = value.astype(BF16)
        return 0

    lax.fori_loop(0, own // ROWS, some, 0)
    both[:own, :] = out[...]
    both[own:, :] = ctr[...]

    @pl.when(pl.program_id(0) == 0)
    def _():
        sums[...] = jnp.zeros_like(sums)

    sums[...] += rowdot(both[...], ctr[...])


def apply_own(orbitals, potential, token, side):
    own, grid, size = orbitals.shape[0], orbitals.shape[1], side * side

    def plane(shift):
        return pl.BlockSpec((own, size), lambda i, at: (0, lax.rem(i + shift + side, side)))

    return call(
        functools.partial(apply_body, side),
        (side,),
        [plane(-1), plane(0), plane(1), pl.BlockSpec((1, size), lambda i, at: (0, i))],
        [plane(0), pl.BlockSpec((2 * own, own), lambda i, at: (0, 0))],
        [jax.ShapeDtypeStruct((own, grid), BF16), jax.ShapeDtypeStruct((2 * own, own), F32)],
        (token, orbitals, orbitals, orbitals, potential),
        scratch=[pltpu.VMEM((2 * own, size), BF16)],
        flops=4 * own * own * grid,
    )


def part_body(side, n, q0, first, last, at, own_ref, applied, pot, *refs):
    refs = list(refs)
    rems, olds, recent = refs[: n - 1], refs[n - 1 : 2 * n - 2], refs[2 * n - 2 : 3 * n - 3]
    refs = refs[3 * n - 3 :]
    before = None if first else refs.pop(0)
    outs, (ring, every, moved, total) = refs[:-4], refs[-4:]
    own = own_ref.shape[0]
    i = pl.program_id(0)

    @pl.when(i == 0)
    def _():
        for j in range(n - 1):
            rows = pl.ds(j * own, own)
            ring[(q0 - 2) % 3, rows, :] = olds[j][...]
            ring[(q0 - 1) % 3, rows, :] = recent[j][...]
        total[...] = jnp.zeros_like(total) if first else before[...]

    slot = lax.rem(q0 + i, 3)
    here = lax.rem(q0 + i + 2, 3)
    back = lax.rem(q0 + i + 1, 3)
    for j in range(n - 1):
        ring[slot, pl.ds(j * own, own), :] = rems[j][...]
    every[:own, :] = own_ref[...]
    moved[:own, :] = applied[...]

    def some(r, _):
        rows = pl.ds(r * ROWS, ROWS)
        ctr = ring[here, rows, :]
        value = near(
            ctr.astype(F32), ring[back, rows, :].astype(F32), ring[slot, rows, :].astype(F32), pot[...], side
        )
        there = pl.ds(pl.multiple_of(own + r * ROWS, ROWS), ROWS)
        every[there, :] = ctr
        moved[there, :] = value.astype(BF16)
        return 0

    lax.fori_loop(0, (n - 1) * own // ROWS, some, 0)
    total[...] += rowdot(moved[...], every[...])

    @pl.when(i == pl.num_programs(0) - 1)
    def _():
        if not last:
            outs[0][...] = total[...]
        else:
            for j in range(n):
                rows = total[((n - j) % n) * own : ((n - j) % n) * own + own, :]
                outs[j][...] = pltpu.roll(rows, j * own, 1) if j else rows


def part(orbitals, applied, potential, at, rems, previous, before, q0, width, last, side):
    own, size, n = orbitals.shape[0], side * side, len(rems) + 1
    total = n * own
    held = previous[0].shape[1] // size

    def plane():
        return pl.BlockSpec((own, size), lambda i, at: (0, lax.rem(at[0] + q0 + i - 2 + side, side)))

    def fixed(shape, column=0):
        return pl.BlockSpec(shape, lambda i, at: (0, column))

    first = before is None
    args = [at, orbitals, applied, potential, *rems, *previous, *previous] + ([] if first else [before])
    specs = [plane(), plane(), pl.BlockSpec((1, size), lambda i, at: (0, lax.rem(at[0] + q0 + i - 2 + side, side)))]
    specs += [pl.BlockSpec((own, size), lambda i, at: (0, i))] * (n - 1)
    specs += [fixed((own, size), held - 2)] * (n - 1) + [fixed((own, size), held - 1)] * (n - 1)
    specs += [] if first else [fixed((total, total))]
    shapes = [(own, total)] * n if last else [(total, total)]
    return call(
        functools.partial(part_body, side, n, q0, first, last),
        (width,),
        specs,
        [fixed(s) for s in shapes],
        [jax.ShapeDtypeStruct(s, F32) for s in shapes],
        tuple(args),
        scratch=[
            pltpu.VMEM((3, (n - 1) * own, size), BF16),
            pltpu.VMEM((total, size), BF16),
            pltpu.VMEM((total, size), BF16),
            pltpu.VMEM((total, total), F32),
        ],
        flops=2 * total * total * size * width,
        limit=32,
    )


def coef_body(n, at, sums, mine, *refs):
    got, (projected, coef, work) = refs[: n - 1], refs[n - 1 :]
    own = mine.shape[0]
    other = mine[:, own:]
    for g in got:
        other = other + g[...]
    work[:, :own] = sums[:own, :]
    work[:, own:] = other
    gram = sums[own:, :]
    same = lax.broadcasted_iota(jnp.int32, gram.shape, 0) == lax.broadcasted_iota(jnp.int32, gram.shape, 1)
    diagonal = jnp.sum(jnp.where(same, gram, 0.0), axis=1, keepdims=True)
    value = work[...]
    coef[...] = (value / diagonal).astype(BF16)
    projected[...] = pltpu.roll(value, at[0] * own, 1)


def coefficients(at, sums, mine, got):
    own, total = mine.shape
    n = total // own

    def whole(x):
        return pl.BlockSpec(x.shape, lambda i, at: (0, 0))

    shape = jax.ShapeDtypeStruct((own, total), F32)
    return call(
        functools.partial(coef_body, n),
        (1,),
        [whole(sums), whole(mine)] + [whole(g) for g in got],
        [whole(shape), whole(shape)],
        [shape, jax.ShapeDtypeStruct((own, total), BF16)],
        (at, sums, mine, *got),
        scratch=[pltpu.VMEM((own, total), F32)],
        limit=16,
    )


def rest_body(n, first, last, at, coef, own_ref, applied, *refs):
    refs = list(refs)
    rems, refs = refs[: n - 1], refs[n - 1 :]
    if not first:
        before, refs = refs[1], refs[2:]
    out, gram, every = refs
    own = own_ref.shape[0]
    i = pl.program_id(0)
    every[:own, :] = own_ref[...]
    for j in range(n - 1):
        every[(j + 1) * own : (j + 2) * own, :] = rems[j][...]
    mixed = jnp.dot(coef[...], every[...], preferred_element_type=F32)
    out[...] = (applied[...].astype(F32) - mixed).astype(BF16)

    @pl.when(i == 0)
    def _():
        gram[...] = jnp.zeros_like(gram) if first else before[...]

    gram[...] += rowdot(own_ref[...], every[...])
    if last:

        @pl.when(i == pl.num_programs(0) - 1)
        def _():
            gram[...] = pltpu.roll(gram[...], at[1] * own, 1)


def rest(at, coef, orbitals, applied, rems, carry, q0, width, last, side):
    own, grid, size, n = orbitals.shape[0], orbitals.shape[1], side * side, len(rems) + 1
    total = n * own

    def plane():
        return pl.BlockSpec((own, size), lambda i, at: (0, lax.rem(at[0] + q0 + i - 1 + side, side)))

    def fixed(shape):
        return pl.BlockSpec(shape, lambda i, at: (0, 0))

    first = carry is None
    args = [at, coef, orbitals, applied, *rems]
    specs = [fixed((own, total)), plane(), plane()]
    specs += [pl.BlockSpec((own, size), lambda i, at: (0, i))] * (n - 1)
    aliases = {}
    if not first:
        aliases = {len(args): 0}
        args += list(carry)
        specs += [pl.BlockSpec(memory_space=ANY), fixed((own, total))]
    return call(
        functools.partial(rest_body, n, first, last),
        (width,),
        specs,
        [plane(), fixed((own, total))],
        [jax.ShapeDtypeStruct((own, grid), BF16), jax.ShapeDtypeStruct((own, total), F32)],
        tuple(args),
        scratch=[pltpu.VMEM((total, size), BF16)],
        aliases=aliases,
        flops=4 * own * total * size * width,
        limit=16,
    )


def cuts(count):
    out = []
    while count:
        out.append(max(1, count // 2))
        count -= out[-1]
    return out


def plan(n, side):
    share = side // n
    widths = [2] + ([share - share // 2, share // 2] if share >= 4 else [share])
    widths.append((side - share - 2) // 4)
    after = cuts(side - sum(widths))
    starts = [sum((widths + after)[:c]) for c in range(len(widths + after))]
    both = list(zip(starts, widths + after))
    return both[: len(widths)], both[len(widths) :]


def shards(n, orbitals, potential):
    own, grid = orbitals.shape
    side = round(grid ** (1 / 3))
    share = side // n
    me = lax.axis_index("band")
    potential = potential.reshape(1, grid)

    def sent(q0, width):
        got = []
        for j in range(1, n):
            dest = lax.rem(me + n - j, n)
            start = lax.rem(dest * share + q0 - 1 + side, side).astype(jnp.int32).reshape(1)
            chunk = pack(orbitals, start, width, side)
            got.append(lax.ppermute(chunk, "band", [(k, (k - j) % n) for k in range(n)]))
        return got

    early, late = plan(n, side)
    at = jnp.stack([me * share, me]).astype(jnp.int32)
    chunks = [(q0, w, sent(q0, w)) for q0, w in early]
    applied, sums = apply_own(orbitals, potential, at, side)
    before = None
    for c in range(1, len(early) - 1):
        q0, w, rems = chunks[c]
        before = part(
            orbitals, applied, potential, at, rems, chunks[c - 1][2],
            None if before is None else before[0], q0, w, c == len(early) - 2, side,
        )
    mine, others = before[0], before[1:]
    got = []
    for j in range(1, n):
        perm = [(k, (k - j) % n) for k in range(n)]
        got.append(lax.ppermute(others[j - 1][:, own:], "band", perm))
    chunks += [(q0, w, sent(q0, w)) for q0, w in late]
    projected, coef = coefficients(at[1:], sums, mine, got)
    carry = None
    for c, (q0, w, rems) in enumerate(chunks):
        carry = rest(at, coef, orbitals, applied, rems, carry, q0, w, c == len(chunks) - 1, side)
    residuals, margin = carry
    return margin, projected, residuals


def solution(mesh):
    n, spec = mesh.shape["band"], P(("frag", "band"), None)

    def body(orbitals, potential):
        return shards(n, orbitals, potential)

    return jax.shard_map(
        body,
        mesh=mesh,
        in_specs=(spec, P("frag")),
        out_specs=(spec, spec, spec),
        check_vma=False,
    )
```

```python
import functools

import jax
import jax.numpy as jnp
from jax import lax
from jax.experimental import pallas as pl
from jax.experimental.pallas import tpu as pltpu
from jax.sharding import PartitionSpec as P


ROWS = 16
WHOLE = 2**20
F32 = jnp.float32
BF16 = jnp.bfloat16
ANY = pl.ANY


def call(kernel, grid, in_specs, out_specs, out_shape, args, scratch=(), aliases={}, flops=0, limit=58):
    args = [pltpu.with_memory_space_constraint(a, pltpu.HBM) if a.size >= WHOLE else a for a in args]
    touched = sum(a.size * a.dtype.itemsize for a in args)
    return pl.pallas_call(
        kernel,
        out_shape=out_shape,
        grid_spec=pltpu.PrefetchScalarGridSpec(
            num_scalar_prefetch=1, grid=grid, in_specs=in_specs, out_specs=out_specs, scratch_shapes=scratch
        ),
        input_output_aliases=aliases,
        compiler_params=pltpu.CompilerParams(
            dimension_semantics=("arbitrary",), vmem_limit_bytes=limit * 2**20
        ),
        cost_estimate=pl.CostEstimate(flops=flops, bytes_accessed=touched, transcendentals=0),
    )(*args)


def near(ctr, left, right, pot, side):
    size = side * side
    z = lax.broadcasted_iota(jnp.int32, ctr.shape, 1) % side
    low = jnp.where(z == 0, pltpu.roll(ctr, size - side + 1, 1), pltpu.roll(ctr, 1, 1))
    high = jnp.where(z == side - 1, pltpu.roll(ctr, side - 1, 1), pltpu.roll(ctr, size - 1, 1))
    beside = (left + right) + (pltpu.roll(ctr, side, 1) + pltpu.roll(ctr, size - side, 1)) + (low + high)
    return (3.0 + pot) * ctr - 0.5 * beside


def rowdot(a, b):
    return lax.dot_general(a, b, (((1,), (1,)), ((), ())), preferred_element_type=F32)


def pack_body(at, src, dst):
    dst[...] = src[...]


def pack(orbitals, start, width, side):
    own, size = orbitals.shape[0], side * side
    return call(
        pack_body,
        (width,),
        [pl.BlockSpec((own, size), lambda i, at: (0, lax.rem(at[0] + i, side)))],
        pl.BlockSpec((own, size), lambda i, at: (0, i)),
        jax.ShapeDtypeStruct((own, width * size), BF16),
        (start, orbitals),
    )


def grab_body(width, size, side, at, src, dst, sems):
    copies = []
    for i in range(width):
        column = pl.multiple_of(lax.rem(at[0] + i, side) * size, size)
        copies.append(
            pltpu.make_async_copy(src.at[:, pl.ds(column, size)], dst.at[:, pl.ds(i * size, size)], sems.at[i])
        )
    for copy in copies:
        copy.start()
    for copy in copies:
        copy.wait()


def grab(orbitals, start, width, side):
    own, size = orbitals.shape[0], side * side
    return call(
        functools.partial(grab_body, width, size, side),
        (1,),
        [pl.BlockSpec(memory_space=ANY)],
        pl.BlockSpec(memory_space=pltpu.VMEM),
        pltpu.VMEM((own, width * size), BF16),
        (start, orbitals),
        scratch=[pltpu.SemaphoreType.DMA((width,))],
    )


def apply_body(side, at, left, ctr, right, pot, out, sums, both):
    own = ctr.shape[0]

    def some(r, _):
        rows = pl.ds(r * ROWS, ROWS)
        value = near(
            ctr[rows, :].astype(F32), left[rows, :].astype(F32), right[rows, :].astype(F32), pot[...], side
        )
        out[rows, :] = value.astype(BF16)
        return 0

    lax.fori_loop(0, own // ROWS, some, 0)
    both[:own, :] = out[...]
    both[own:, :] = ctr[...]

    @pl.when(pl.program_id(0) == 0)
    def _():
        sums[...] = jnp.zeros_like(sums)

    sums[...] += rowdot(both[...], ctr[...])


def apply_own(orbitals, potential, token, side):
    own, grid, size = orbitals.shape[0], orbitals.shape[1], side * side

    def plane(shift):
        return pl.BlockSpec((own, size), lambda i, at: (0, lax.rem(i + shift + side, side)))

    return call(
        functools.partial(apply_body, side),
        (side,),
        [plane(-1), plane(0), plane(1), pl.BlockSpec((1, size), lambda i, at: (0, i))],
        [plane(0), pl.BlockSpec((2 * own, own), lambda i, at: (0, 0))],
        [jax.ShapeDtypeStruct((own, grid), BF16), jax.ShapeDtypeStruct((2 * own, own), F32)],
        (token, orbitals, orbitals, orbitals, potential),
        scratch=[pltpu.VMEM((2 * own, size), BF16)],
        flops=4 * own * own * grid,
    )


def part_body(side, n, q0, first, last, at, own_ref, applied, pot, *refs):
    refs = list(refs)
    rems, olds, recent = refs[: n - 1], refs[n - 1 : 2 * n - 2], refs[2 * n - 2 : 3 * n - 3]
    refs = refs[3 * n - 3 :]
    before = None if first else refs.pop(0)
    outs, (ring, every, moved, total) = refs[:-4], refs[-4:]
    own = own_ref.shape[0]
    i = pl.program_id(0)

    @pl.when(i == 0)
    def _():
        for j in range(n - 1):
            rows = pl.ds(j * own, own)
            ring[(q0 - 2) % 3, rows, :] = olds[j][...]
            ring[(q0 - 1) % 3, rows, :] = recent[j][...]
        total[...] = jnp.zeros_like(total) if first else before[...]

    slot = lax.rem(q0 + i, 3)
    here = lax.rem(q0 + i + 2, 3)
    back = lax.rem(q0 + i + 1, 3)
    for j in range(n - 1):
        ring[slot, pl.ds(j * own, own), :] = rems[j][...]
    every[:own, :] = own_ref[...]
    moved[:own, :] = applied[...]

    def some(r, _):
        rows = pl.ds(r * ROWS, ROWS)
        ctr = ring[here, rows, :]
        value = near(
            ctr.astype(F32), ring[back, rows, :].astype(F32), ring[slot, rows, :].astype(F32), pot[...], side
        )
        there = pl.ds(pl.multiple_of(own + r * ROWS, ROWS), ROWS)
        every[there, :] = ctr
        moved[there, :] = value.astype(BF16)
        return 0

    lax.fori_loop(0, (n - 1) * own // ROWS, some, 0)
    total[...] += rowdot(moved[...], every[...])

    @pl.when(i == pl.num_programs(0) - 1)
    def _():
        if not last:
            outs[0][...] = total[...]
        else:
            for j in range(n):
                rows = total[((n - j) % n) * own : ((n - j) % n) * own + own, :]
                outs[j][...] = pltpu.roll(rows, j * own, 1) if j else rows


def part(orbitals, applied, potential, at, rems, previous, before, q0, width, last, side):
    own, size, n = orbitals.shape[0], side * side, len(rems) + 1
    total = n * own
    held = previous[0].shape[1] // size

    def plane():
        return pl.BlockSpec((own, size), lambda i, at: (0, lax.rem(at[0] + q0 + i - 2 + side, side)))

    def fixed(shape, column=0):
        return pl.BlockSpec(shape, lambda i, at: (0, column))

    first = before is None
    args = [at, orbitals, applied, potential, *rems, *previous, *previous] + ([] if first else [before])
    specs = [plane(), plane(), pl.BlockSpec((1, size), lambda i, at: (0, lax.rem(at[0] + q0 + i - 2 + side, side)))]
    specs += [pl.BlockSpec((own, size), lambda i, at: (0, i))] * (n - 1)
    specs += [fixed((own, size), held - 2)] * (n - 1) + [fixed((own, size), held - 1)] * (n - 1)
    specs += [] if first else [fixed((total, total))]
    shapes = [(own, total)] * n if last else [(total, total)]
    return call(
        functools.partial(part_body, side, n, q0, first, last),
        (width,),
        specs,
        [fixed(s) for s in shapes],
        [jax.ShapeDtypeStruct(s, F32) for s in shapes],
        tuple(args),
        scratch=[
            pltpu.VMEM((3, (n - 1) * own, size), BF16),
            pltpu.VMEM((total, size), BF16),
            pltpu.VMEM((total, size), BF16),
            pltpu.VMEM((total, total), F32),
        ],
        flops=2 * total * total * size * width,
        limit=32,
    )


def coef_body(n, at, sums, mine, *refs):
    got, (projected, coef, work) = refs[: n - 1], refs[n - 1 :]
    own = mine.shape[0]
    other = mine[:, own:]
    for g in got:
        other = other + g[...]
    work[:, :own] = sums[:own, :]
    work[:, own:] = other
    gram = sums[own:, :]
    same = lax.broadcasted_iota(jnp.int32, gram.shape, 0) == lax.broadcasted_iota(jnp.int32, gram.shape, 1)
    diagonal = jnp.sum(jnp.where(same, gram, 0.0), axis=1, keepdims=True)
    value = work[...]
    coef[...] = (value / diagonal).astype(BF16)
    projected[...] = pltpu.roll(value, at[0] * own, 1)


def coefficients(at, sums, mine, got):
    own, total = mine.shape
    n = total // own

    def whole(x):
        return pl.BlockSpec(x.shape, lambda i, at: (0, 0))

    shape = jax.ShapeDtypeStruct((own, total), F32)
    return call(
        functools.partial(coef_body, n),
        (1,),
        [whole(sums), whole(mine)] + [whole(g) for g in got],
        [whole(shape), whole(shape)],
        [shape, jax.ShapeDtypeStruct((own, total), BF16)],
        (at, sums, mine, *got),
        scratch=[pltpu.VMEM((own, total), F32)],
        limit=16,
    )


def rest_body(n, first, last, at, coef, own_ref, applied, *refs):
    refs = list(refs)
    rems, refs = refs[: n - 1], refs[n - 1 :]
    if not first:
        before, refs = refs[1], refs[2:]
    out, gram, every = refs
    own = own_ref.shape[0]
    i = pl.program_id(0)
    every[:own, :] = own_ref[...]
    for j in range(n - 1):
        every[(j + 1) * own : (j + 2) * own, :] = rems[j][...]
    mixed = jnp.dot(coef[...], every[...], preferred_element_type=F32)
    out[...] = (applied[...].astype(F32) - mixed).astype(BF16)

    @pl.when(i == 0)
    def _():
        gram[...] = jnp.zeros_like(gram) if first else before[...]

    gram[...] += rowdot(own_ref[...], every[...])
    if last:

        @pl.when(i == pl.num_programs(0) - 1)
        def _():
            gram[...] = pltpu.roll(gram[...], at[1] * own, 1)


def rest(at, coef, orbitals, applied, rems, carry, q0, width, last, side):
    own, grid, size, n = orbitals.shape[0], orbitals.shape[1], side * side, len(rems) + 1
    total = n * own

    def plane():
        return pl.BlockSpec((own, size), lambda i, at: (0, lax.rem(at[0] + q0 + i - 1 + side, side)))

    def fixed(shape):
        return pl.BlockSpec(shape, lambda i, at: (0, 0))

    first = carry is None
    args = [at, coef, orbitals, applied, *rems]
    specs = [fixed((own, total)), plane(), plane()]
    specs += [pl.BlockSpec((own, size), lambda i, at: (0, i))] * (n - 1)
    aliases = {}
    if not first:
        aliases = {len(args): 0}
        args += list(carry)
        specs += [pl.BlockSpec(memory_space=ANY), fixed((own, total))]
    return call(
        functools.partial(rest_body, n, first, last),
        (width,),
        specs,
        [plane(), fixed((own, total))],
        [jax.ShapeDtypeStruct((own, grid), BF16), jax.ShapeDtypeStruct((own, total), F32)],
        tuple(args),
        scratch=[pltpu.VMEM((total, size), BF16)],
        aliases=aliases,
        flops=4 * own * total * size * width,
        limit=16,
    )


def cuts(count):
    out = []
    while count:
        out.append(max(1, count // 2))
        count -= out[-1]
    return out


def plan(n, side):
    share = side // n
    short = max(2, share // 4)
    widths = [2] + ([share - short, short] if share >= 4 else [share])
    widths.append((side - share - 2) // 3)
    after = cuts(side - sum(widths))
    starts = [sum((widths + after)[:c]) for c in range(len(widths + after))]
    both = list(zip(starts, widths + after))
    return both[: len(widths)], both[len(widths) :]


def shards(n, orbitals, potential):
    own, grid = orbitals.shape
    side = round(grid ** (1 / 3))
    share = side // n
    me = lax.axis_index("band")
    potential = potential.reshape(1, grid)

    def sent(c, q0, width):
        got = []
        for j in range(1, n):
            dest = lax.rem(me + n - j, n)
            start = lax.rem(dest * share + q0 - 1 + side, side).astype(jnp.int32).reshape(1)
            chunk = (pack if c else grab)(orbitals, start, width, side)
            got.append(lax.ppermute(chunk, "band", [(k, (k - j) % n) for k in range(n)]))
        return got

    early, late = plan(n, side)
    at = jnp.stack([me * share, me]).astype(jnp.int32)
    chunks = [(q0, w, sent(c, q0, w)) for c, (q0, w) in enumerate(early)]
    applied, sums = apply_own(orbitals, potential, at, side)
    before = None
    for c in range(1, len(early) - 1):
        q0, w, rems = chunks[c]
        before = part(
            orbitals, applied, potential, at, rems, chunks[c - 1][2],
            None if before is None else before[0], q0, w, c == len(early) - 2, side,
        )
    mine, others = before[0], before[1:]
    got = []
    for j in range(1, n):
        perm = [(k, (k - j) % n) for k in range(n)]
        got.append(lax.ppermute(others[j - 1][:, own:], "band", perm))
    chunks += [(q0, w, sent(len(early) + c, q0, w)) for c, (q0, w) in enumerate(late)]
    projected, coef = coefficients(at[1:], sums, mine, got)
    carry = None
    for c, (q0, w, rems) in enumerate(chunks):
        carry = rest(at, coef, orbitals, applied, rems, carry, q0, w, c == len(chunks) - 1, side)
    residuals, margin = carry
    return margin, projected, residuals


def solution(mesh):
    n, spec = mesh.shape["band"], P(("frag", "band"), None)

    def body(orbitals, potential):
        return shards(n, orbitals, potential)

    return jax.shard_map(
        body,
        mesh=mesh,
        in_specs=(spec, P("frag")),
        out_specs=(spec, spec, spec),
        check_vma=False,
    )
```

```python
import functools

import jax
import jax.numpy as jnp
from jax import lax
from jax.experimental import pallas as pl
from jax.experimental.pallas import tpu as pltpu
from jax.sharding import PartitionSpec as P


ROWS = 16
WHOLE = 2**20
PARTS = 2
F32 = jnp.float32
BF16 = jnp.bfloat16
ANY = pl.ANY


def call(kernel, grid, in_specs, out_specs, out_shape, args, scratch=(), aliases={}, flops=0, limit=58, keep=True):
    if keep:
        args = [pltpu.with_memory_space_constraint(a, pltpu.HBM) if a.size >= WHOLE else a for a in args]
    touched = sum(a.size * a.dtype.itemsize for a in args)
    return pl.pallas_call(
        kernel,
        out_shape=out_shape,
        grid_spec=pltpu.PrefetchScalarGridSpec(
            num_scalar_prefetch=1, grid=grid, in_specs=in_specs, out_specs=out_specs, scratch_shapes=scratch
        ),
        input_output_aliases=aliases,
        compiler_params=pltpu.CompilerParams(
            dimension_semantics=("arbitrary",), vmem_limit_bytes=limit * 2**20
        ),
        cost_estimate=pl.CostEstimate(flops=flops, bytes_accessed=touched, transcendentals=0),
    )(*args)


def near(ctr, left, right, pot, side):
    size = side * side
    z = lax.broadcasted_iota(jnp.int32, ctr.shape, 1) % side
    low = jnp.where(z == 0, pltpu.roll(ctr, size - side + 1, 1), pltpu.roll(ctr, 1, 1))
    high = jnp.where(z == side - 1, pltpu.roll(ctr, side - 1, 1), pltpu.roll(ctr, size - 1, 1))
    beside = (left + right) + (pltpu.roll(ctr, side, 1) + pltpu.roll(ctr, size - side, 1)) + (low + high)
    return (3.0 + pot) * ctr - 0.5 * beside


def rowdot(a, b):
    return lax.dot_general(a, b, (((1,), (1,)), ((), ())), preferred_element_type=F32)


def pack_body(at, src, dst):
    dst[...] = src[...]


def pack(orbitals, start, width, size):
    own, count = orbitals.shape[0], orbitals.shape[1] // size
    return call(
        pack_body,
        (width,),
        [pl.BlockSpec((own, size), lambda i, at: (0, lax.rem(at[0] + i, count)))],
        pl.BlockSpec((own, size), lambda i, at: (0, i)),
        jax.ShapeDtypeStruct((own, width * size), BF16),
        (start, orbitals),
    )


def grab_body(width, size, count, at, src, dst, sems):
    copies = []
    for i in range(width):
        column = pl.multiple_of(lax.rem(at[0] + i, count) * size, size)
        copies.append(
            pltpu.make_async_copy(src.at[:, pl.ds(column, size)], dst.at[:, pl.ds(i * size, size)], sems.at[i])
        )
    for copy in copies:
        copy.start()
    for copy in copies:
        copy.wait()


def grab(orbitals, start, width, size):
    own, count = orbitals.shape[0], orbitals.shape[1] // size
    return call(
        functools.partial(grab_body, width, size, count),
        (1,),
        [pl.BlockSpec(memory_space=ANY)],
        pl.BlockSpec(memory_space=pltpu.VMEM),
        pltpu.VMEM((own, width * size), BF16),
        (start, orbitals),
        scratch=[pltpu.SemaphoreType.DMA((width,))],
    )


def apply_body(side, at, left, ctr, right, pot, out, sums, both):
    own = ctr.shape[0]

    def some(r, _):
        rows = pl.ds(r * ROWS, ROWS)
        value = near(
            ctr[rows, :].astype(F32), left[rows, :].astype(F32), right[rows, :].astype(F32), pot[...], side
        )
        out[rows, :] = value.astype(BF16)
        return 0

    lax.fori_loop(0, own // ROWS, some, 0)
    both[:own, :] = out[...]
    both[own:, :] = ctr[...]

    @pl.when(pl.program_id(0) == 0)
    def _():
        sums[...] = jnp.zeros_like(sums)

    sums[...] += rowdot(both[...], ctr[...])


def apply_own(orbitals, potential, token, side):
    own, grid, size = orbitals.shape[0], orbitals.shape[1], side * side

    def plane(shift):
        return pl.BlockSpec((own, size), lambda i, at: (0, lax.rem(i + shift + side, side)))

    return call(
        functools.partial(apply_body, side),
        (side,),
        [plane(-1), plane(0), plane(1), pl.BlockSpec((1, size), lambda i, at: (0, i))],
        [plane(0), pl.BlockSpec((2 * own, own), lambda i, at: (0, 0))],
        [jax.ShapeDtypeStruct((own, grid), BF16), jax.ShapeDtypeStruct((2 * own, own), F32)],
        (token, orbitals, orbitals, orbitals, potential),
        scratch=[pltpu.VMEM((2 * own, size), BF16)],
        flops=4 * own * own * grid,
    )


def part_body(side, n, q0, first, last, at, own_ref, applied, pot, *refs):
    refs = list(refs)
    rems, olds, recent = refs[: n - 1], refs[n - 1 : 2 * n - 2], refs[2 * n - 2 : 3 * n - 3]
    refs = refs[3 * n - 3 :]
    before = None if first else refs.pop(0)
    outs, (ring, every, moved, total) = refs[:-4], refs[-4:]
    own = own_ref.shape[0]
    i = pl.program_id(0)

    @pl.when(i == 0)
    def _():
        for j in range(n - 1):
            rows = pl.ds(j * own, own)
            ring[(q0 - 2) % 3, rows, :] = olds[j][...]
            ring[(q0 - 1) % 3, rows, :] = recent[j][...]
        total[...] = jnp.zeros_like(total) if first else before[...]

    slot = lax.rem(q0 + i, 3)
    here = lax.rem(q0 + i + 2, 3)
    back = lax.rem(q0 + i + 1, 3)
    for j in range(n - 1):
        ring[slot, pl.ds(j * own, own), :] = rems[j][...]
    every[:own, :] = own_ref[...]
    moved[:own, :] = applied[...]

    def some(r, _):
        rows = pl.ds(r * ROWS, ROWS)
        ctr = ring[here, rows, :]
        value = near(
            ctr.astype(F32), ring[back, rows, :].astype(F32), ring[slot, rows, :].astype(F32), pot[...], side
        )
        there = pl.ds(pl.multiple_of(own + r * ROWS, ROWS), ROWS)
        every[there, :] = ctr
        moved[there, :] = value.astype(BF16)
        return 0

    lax.fori_loop(0, (n - 1) * own // ROWS, some, 0)
    total[...] += rowdot(moved[...], every[...])

    @pl.when(i == pl.num_programs(0) - 1)
    def _():
        if not last:
            outs[0][...] = total[...]
        else:
            for j in range(n):
                rows = total[((n - j) % n) * own : ((n - j) % n) * own + own, :]
                outs[j][...] = pltpu.roll(rows, j * own, 1) if j else rows


def part(orbitals, applied, potential, at, rems, previous, before, q0, width, last, side):
    own, size, n = orbitals.shape[0], side * side, len(rems) + 1
    total = n * own
    held = previous[0].shape[1] // size

    def plane():
        return pl.BlockSpec((own, size), lambda i, at: (0, lax.rem(at[0] + q0 + i - 2 + side, side)))

    def fixed(shape, column=0):
        return pl.BlockSpec(shape, lambda i, at: (0, column))

    first = before is None
    args = [at, orbitals, applied, potential, *rems, *previous, *previous] + ([] if first else [before])
    specs = [plane(), plane(), pl.BlockSpec((1, size), lambda i, at: (0, lax.rem(at[0] + q0 + i - 2 + side, side)))]
    specs += [pl.BlockSpec((own, size), lambda i, at: (0, i))] * (n - 1)
    specs += [fixed((own, size), held - 2)] * (n - 1) + [fixed((own, size), held - 1)] * (n - 1)
    specs += [] if first else [fixed((total, total))]
    shapes = [(own, total)] * n if last else [(total, total)]
    return call(
        functools.partial(part_body, side, n, q0, first, last),
        (width,),
        specs,
        [fixed(s) for s in shapes],
        [jax.ShapeDtypeStruct(s, F32) for s in shapes],
        tuple(args),
        scratch=[
            pltpu.VMEM((3, (n - 1) * own, size), BF16),
            pltpu.VMEM((total, size), BF16),
            pltpu.VMEM((total, size), BF16),
            pltpu.VMEM((total, total), F32),
        ],
        flops=2 * total * total * size * width,
        limit=32,
    )


def coef_body(n, at, sums, mine, *refs):
    got, (projected, coef, work) = refs[: n - 1], refs[n - 1 :]
    own = mine.shape[0]
    other = mine[:, own:]
    for g in got:
        other = other + g[...]
    work[:, :own] = sums[:own, :]
    work[:, own:] = other
    gram = sums[own:, :]
    same = lax.broadcasted_iota(jnp.int32, gram.shape, 0) == lax.broadcasted_iota(jnp.int32, gram.shape, 1)
    diagonal = jnp.sum(jnp.where(same, gram, 0.0), axis=1, keepdims=True)
    value = work[...]
    coef[...] = (value / diagonal).astype(BF16)
    projected[...] = pltpu.roll(value, at[0] * own, 1)


def coefficients(at, sums, mine, got):
    own, total = mine.shape
    n = total // own

    def whole(x):
        return pl.BlockSpec(x.shape, lambda i, at: (0, 0))

    shape = jax.ShapeDtypeStruct((own, total), F32)
    return call(
        functools.partial(coef_body, n),
        (1,),
        [whole(sums), whole(mine)] + [whole(g) for g in got],
        [whole(shape), whole(shape)],
        [shape, jax.ShapeDtypeStruct((own, total), BF16)],
        (at, sums, mine, *got),
        scratch=[pltpu.VMEM((own, total), F32)],
        limit=16,
    )


def rest_body(n, first, last, at, coef, own_ref, applied, *refs):
    refs = list(refs)
    rems, refs = refs[: n - 1], refs[n - 1 :]
    if not first:
        before, refs = refs[1], refs[2:]
    out, gram, every = refs
    own = own_ref.shape[0]
    i = pl.program_id(0)
    every[:own, :] = own_ref[...]
    for j in range(n - 1):
        every[(j + 1) * own : (j + 2) * own, :] = rems[j][...]
    mixed = jnp.dot(coef[...], every[...], preferred_element_type=F32)
    out[...] = (applied[...].astype(F32) - mixed).astype(BF16)

    @pl.when(i == 0)
    def _():
        gram[...] = jnp.zeros_like(gram) if first else before[...]

    gram[...] += rowdot(own_ref[...], every[...])
    if last:

        @pl.when(i == pl.num_programs(0) - 1)
        def _():
            gram[...] = pltpu.roll(gram[...], at[1] * own, 1)


def rest(at, coef, orbitals, applied, rems, carry, q0, width, last, size, ratio):
    own, grid, n = orbitals.shape[0], orbitals.shape[1], len(rems) + 1
    total, count = n * own, grid // size

    def plane():
        return pl.BlockSpec((own, size), lambda i, at: (0, lax.rem((at[0] - 1) * ratio + q0 + i + count, count)))

    def fixed(shape):
        return pl.BlockSpec(shape, lambda i, at: (0, 0))

    first = carry is None
    args = [at, coef, orbitals, applied, *rems]
    specs = [fixed((own, total)), plane(), plane()]
    specs += [pl.BlockSpec((own, size), lambda i, at: (0, i))] * (n - 1)
    aliases = {}
    if not first:
        aliases = {len(args): 0}
        args += list(carry)
        specs += [pl.BlockSpec(memory_space=ANY), fixed((own, total))]
    return call(
        functools.partial(rest_body, n, first, last),
        (width,),
        specs,
        [plane(), fixed((own, total))],
        [jax.ShapeDtypeStruct((own, grid), BF16), jax.ShapeDtypeStruct((own, total), F32)],
        tuple(args),
        scratch=[pltpu.VMEM((total, size), BF16)],
        aliases=aliases,
        flops=4 * own * total * size * width,
        keep=False,
        limit=16,
    )


def cuts(count):
    out = []
    while count:
        out.append(max(1, count // 2))
        count -= out[-1]
    return out


def plan(n, side):
    share = side // n
    short = max(2, share // 4)
    widths = [2] + ([share - short, short] if share >= 4 else [share])
    widths.append((side - share - 2) // 3)
    after = cuts(PARTS * (side - sum(widths)))
    early = [(sum(widths[:c]), w, 1) for c, w in enumerate(widths)]
    late = [(PARTS * sum(widths) + sum(after[:c]), w, PARTS) for c, w in enumerate(after)]
    return early, late


def shards(n, orbitals, potential):
    own, grid = orbitals.shape
    side = round(grid ** (1 / 3))
    share = side // n
    me = lax.axis_index("band")
    potential = potential.reshape(1, grid)

    def sent(c, q0, width, ratio):
        got, count = [], side * ratio
        for j in range(1, n):
            dest = lax.rem(me + n - j, n)
            start = lax.rem((dest * share - 1) * ratio + q0 + count, count).astype(jnp.int32).reshape(1)
            chunk = (pack if c else grab)(orbitals, start, width, grid // count)
            got.append(lax.ppermute(chunk, "band", [(k, (k - j) % n) for k in range(n)]))
        return got

    early, late = plan(n, side)
    at = jnp.stack([me * share, me]).astype(jnp.int32)
    chunks = [(*block, sent(c, *block)) for c, block in enumerate(early)]
    applied, sums = apply_own(orbitals, potential, at, side)
    before = None
    for c in range(1, len(early) - 1):
        q0, w, _, rems = chunks[c]
        before = part(
            orbitals, applied, potential, at, rems, chunks[c - 1][3],
            None if before is None else before[0], q0, w, c == len(early) - 2, side,
        )
    mine, others = before[0], before[1:]
    got = []
    for j in range(1, n):
        perm = [(k, (k - j) % n) for k in range(n)]
        got.append(lax.ppermute(others[j - 1][:, own:], "band", perm))
    chunks += [(*block, sent(len(early) + c, *block)) for c, block in enumerate(late)]
    projected, coef = coefficients(at[1:], sums, mine, got)
    carry = None
    for c, (q0, w, ratio, rems) in enumerate(chunks):
        last = c == len(chunks) - 1
        carry = rest(at, coef, orbitals, applied, rems, carry, q0, w, last, grid // (side * ratio), ratio)
    residuals, margin = carry
    return margin, projected, residuals


def solution(mesh):
    n, spec = mesh.shape["band"], P(("frag", "band"), None)

    def body(orbitals, potential):
        return shards(n, orbitals, potential)

    return jax.shard_map(
        body,
        mesh=mesh,
        in_specs=(spec, P("frag")),
        out_specs=(spec, spec, spec),
        check_vma=False,
    )
```

```python
import functools

import jax
import jax.numpy as jnp
from jax import lax
from jax.experimental import pallas as pl
from jax.experimental.pallas import tpu as pltpu
from jax.sharding import PartitionSpec as P


ROWS = 16
WHOLE = 2**20
PARTS = 2
F32 = jnp.float32
BF16 = jnp.bfloat16
ANY = pl.ANY


def call(kernel, grid, in_specs, out_specs, out_shape, args, scratch=(), aliases={}, flops=0, limit=16):
    args = [pltpu.with_memory_space_constraint(a, pltpu.HBM) if a.size >= WHOLE else a for a in args]
    touched = sum(a.size * a.dtype.itemsize for a in args)
    return pl.pallas_call(
        kernel,
        out_shape=out_shape,
        grid_spec=pltpu.PrefetchScalarGridSpec(
            num_scalar_prefetch=1, grid=grid, in_specs=in_specs, out_specs=out_specs, scratch_shapes=scratch
        ),
        input_output_aliases=aliases,
        compiler_params=pltpu.CompilerParams(
            dimension_semantics=("arbitrary",), vmem_limit_bytes=limit * 2**20
        ),
        cost_estimate=pl.CostEstimate(flops=flops, bytes_accessed=touched, transcendentals=0),
    )(*args)


def near(ctr, left, right, pot, side):
    size = side * side
    z = lax.broadcasted_iota(jnp.int32, ctr.shape, 1) % side
    low = jnp.where(z == 0, pltpu.roll(ctr, size - side + 1, 1), pltpu.roll(ctr, 1, 1))
    high = jnp.where(z == side - 1, pltpu.roll(ctr, side - 1, 1), pltpu.roll(ctr, size - 1, 1))
    beside = (left + right) + (pltpu.roll(ctr, side, 1) + pltpu.roll(ctr, size - side, 1)) + (low + high)
    return (3.0 + pot) * ctr - 0.5 * beside


def rowdot(a, b):
    return lax.dot_general(a, b, (((1,), (1,)), ((), ())), preferred_element_type=F32)


def pack_body(at, src, dst):
    dst[...] = src[...]


def pack(orbitals, start, width, size):
    own, count = orbitals.shape[0], orbitals.shape[1] // size
    return call(
        pack_body,
        (width,),
        [pl.BlockSpec((own, size), lambda i, at: (0, lax.rem(at[0] + i, count)))],
        pl.BlockSpec((own, size), lambda i, at: (0, i)),
        jax.ShapeDtypeStruct((own, width * size), BF16),
        (start, orbitals),
    )


def grab_body(width, size, count, at, src, dst, sems):
    copies = []
    for i in range(width):
        column = pl.multiple_of(lax.rem(at[0] + i, count) * size, size)
        copies.append(
            pltpu.make_async_copy(src.at[:, pl.ds(column, size)], dst.at[:, pl.ds(i * size, size)], sems.at[i])
        )
    for copy in copies:
        copy.start()
    for copy in copies:
        copy.wait()


def grab(orbitals, start, width, size):
    own, count = orbitals.shape[0], orbitals.shape[1] // size
    return call(
        functools.partial(grab_body, width, size, count),
        (1,),
        [pl.BlockSpec(memory_space=ANY)],
        pl.BlockSpec(memory_space=pltpu.VMEM),
        pltpu.VMEM((own, width * size), BF16),
        (start, orbitals),
        scratch=[pltpu.SemaphoreType.DMA((width,))],
    )


def apply_body(side, at, left, ctr, right, pot, out, sums, both):
    own = ctr.shape[0]

    def some(r, _):
        rows = pl.ds(r * ROWS, ROWS)
        value = near(
            ctr[rows, :].astype(F32), left[rows, :].astype(F32), right[rows, :].astype(F32), pot[...], side
        )
        out[rows, :] = value.astype(BF16)
        return 0

    lax.fori_loop(0, own // ROWS, some, 0)
    both[:own, :] = out[...]
    both[own:, :] = ctr[...]

    @pl.when(pl.program_id(0) == 0)
    def _():
        sums[...] = jnp.zeros_like(sums)

    sums[...] += rowdot(both[...], ctr[...])


def apply_own(orbitals, potential, token, side):
    own, grid, size = orbitals.shape[0], orbitals.shape[1], side * side

    def plane(shift):
        return pl.BlockSpec((own, size), lambda i, at: (0, lax.rem(i + shift + side, side)))

    return call(
        functools.partial(apply_body, side),
        (side,),
        [plane(-1), plane(0), plane(1), pl.BlockSpec((1, size), lambda i, at: (0, i))],
        [plane(0), pl.BlockSpec((2 * own, own), lambda i, at: (0, 0))],
        [jax.ShapeDtypeStruct((own, grid), BF16), jax.ShapeDtypeStruct((2 * own, own), F32)],
        (token, orbitals, orbitals, orbitals, potential),
        scratch=[pltpu.VMEM((2 * own, size), BF16)],
        flops=4 * own * own * grid,
        limit=56,
    )


def part_body(side, n, q0, first, last, at, own_ref, applied, pot, *refs):
    refs = list(refs)
    rems, olds, recent = refs[: n - 1], refs[n - 1 : 2 * n - 2], refs[2 * n - 2 : 3 * n - 3]
    refs = refs[3 * n - 3 :]
    before = None if first else refs.pop(0)
    outs, (ring, every, moved, total) = refs[:-4], refs[-4:]
    own = own_ref.shape[0]
    i = pl.program_id(0)

    @pl.when(i == 0)
    def _():
        for j in range(n - 1):
            rows = pl.ds(j * own, own)
            ring[(q0 - 2) % 3, rows, :] = olds[j][...]
            ring[(q0 - 1) % 3, rows, :] = recent[j][...]
        total[...] = jnp.zeros_like(total) if first else before[...]

    slot = lax.rem(q0 + i, 3)
    here = lax.rem(q0 + i + 2, 3)
    back = lax.rem(q0 + i + 1, 3)
    for j in range(n - 1):
        ring[slot, pl.ds(j * own, own), :] = rems[j][...]
    every[:own, :] = own_ref[...]
    moved[:own, :] = applied[...]

    def some(r, _):
        rows = pl.ds(r * ROWS, ROWS)
        ctr = ring[here, rows, :]
        value = near(
            ctr.astype(F32), ring[back, rows, :].astype(F32), ring[slot, rows, :].astype(F32), pot[...], side
        )
        there = pl.ds(pl.multiple_of(own + r * ROWS, ROWS), ROWS)
        every[there, :] = ctr
        moved[there, :] = value.astype(BF16)
        return 0

    lax.fori_loop(0, (n - 1) * own // ROWS, some, 0)
    total[...] += rowdot(moved[...], every[...])

    @pl.when(i == pl.num_programs(0) - 1)
    def _():
        if not last:
            outs[0][...] = total[...]
        else:
            for j in range(n):
                rows = total[((n - j) % n) * own : ((n - j) % n) * own + own, :]
                outs[j][...] = pltpu.roll(rows, j * own, 1) if j else rows


def part(orbitals, applied, potential, at, rems, previous, before, q0, width, last, side):
    own, size, n = orbitals.shape[0], side * side, len(rems) + 1
    total = n * own
    held = previous[0].shape[1] // size

    def plane():
        return pl.BlockSpec((own, size), lambda i, at: (0, lax.rem(at[0] + q0 + i - 2 + side, side)))

    def fixed(shape, column=0):
        return pl.BlockSpec(shape, lambda i, at: (0, column))

    first = before is None
    args = [at, orbitals, applied, potential, *rems, *previous, *previous] + ([] if first else [before])
    specs = [plane(), plane(), pl.BlockSpec((1, size), lambda i, at: (0, lax.rem(at[0] + q0 + i - 2 + side, side)))]
    specs += [pl.BlockSpec((own, size), lambda i, at: (0, i))] * (n - 1)
    specs += [fixed((own, size), held - 2)] * (n - 1) + [fixed((own, size), held - 1)] * (n - 1)
    specs += [] if first else [fixed((total, total))]
    shapes = [(own, total)] * n if last else [(total, total)]
    return call(
        functools.partial(part_body, side, n, q0, first, last),
        (width,),
        specs,
        [fixed(s) for s in shapes],
        [jax.ShapeDtypeStruct(s, F32) for s in shapes],
        tuple(args),
        scratch=[
            pltpu.VMEM((3, (n - 1) * own, size), BF16),
            pltpu.VMEM((total, size), BF16),
            pltpu.VMEM((total, size), BF16),
            pltpu.VMEM((total, total), F32),
        ],
        flops=2 * total * total * size * width,
    )


def coef_body(n, at, sums, mine, *refs):
    got, (projected, coef, work) = refs[: n - 1], refs[n - 1 :]
    own = mine.shape[0]
    other = mine[:, own:]
    for g in got:
        other = other + g[...]
    work[:, :own] = sums[:own, :]
    work[:, own:] = other
    gram = sums[own:, :]
    same = lax.broadcasted_iota(jnp.int32, gram.shape, 0) == lax.broadcasted_iota(jnp.int32, gram.shape, 1)
    diagonal = jnp.sum(jnp.where(same, gram, 0.0), axis=1, keepdims=True)
    value = work[...]
    coef[...] = (value / diagonal).astype(BF16)
    projected[...] = pltpu.roll(value, at[0] * own, 1)


def coefficients(at, sums, mine, got):
    own, total = mine.shape
    n = total // own

    def whole(x):
        return pl.BlockSpec(x.shape, lambda i, at: (0, 0))

    shape = jax.ShapeDtypeStruct((own, total), F32)
    return call(
        functools.partial(coef_body, n),
        (1,),
        [whole(sums), whole(mine)] + [whole(g) for g in got],
        [whole(shape), whole(shape)],
        [shape, jax.ShapeDtypeStruct((own, total), BF16)],
        (at, sums, mine, *got),
        scratch=[pltpu.VMEM((own, total), F32)],
    )


def rest_body(n, first, at, coef, own_ref, applied, *refs):
    refs = list(refs)
    rems, refs = refs[: n - 1], refs[n - 1 :]
    if not first:
        before, refs = refs[1], refs[2:]
    out, gram, every = refs
    own = own_ref.shape[0]
    every[:own, :] = own_ref[...]
    for j in range(n - 1):
        every[(j + 1) * own : (j + 2) * own, :] = rems[j][...]
    mixed = jnp.dot(coef[...], every[...], preferred_element_type=F32)
    out[...] = (applied[...].astype(F32) - mixed).astype(BF16)

    @pl.when(pl.program_id(0) == 0)
    def _():
        gram[...] = jnp.zeros_like(gram) if first else before[...]

    gram[...] += rowdot(own_ref[...], every[own:, :])


def rest(at, coef, orbitals, applied, rems, carry, q0, width, size, ratio):
    own, grid, n = orbitals.shape[0], orbitals.shape[1], len(rems) + 1
    total, count = n * own, grid // size

    def plane():
        return pl.BlockSpec((own, size), lambda i, at: (0, lax.rem((at[0] - 1) * ratio + q0 + i + count, count)))

    def fixed(shape):
        return pl.BlockSpec(shape, lambda i, at: (0, 0))

    first = carry is None
    args = [at, coef, orbitals, applied, *rems]
    specs = [fixed((own, total)), plane(), plane()]
    specs += [pl.BlockSpec((own, size), lambda i, at: (0, i))] * (n - 1)
    aliases = {}
    if not first:
        aliases = {len(args): 0}
        args += list(carry)
        specs += [pl.BlockSpec(memory_space=ANY), fixed((own, total - own))]
    return call(
        functools.partial(rest_body, n, first),
        (width,),
        specs,
        [plane(), fixed((own, total - own))],
        [jax.ShapeDtypeStruct((own, grid), BF16), jax.ShapeDtypeStruct((own, total - own), F32)],
        tuple(args),
        scratch=[pltpu.VMEM((total, size), BF16)],
        aliases=aliases,
        flops=4 * own * total * size * width,
    )


def ready_body(at, coef, own_ref, applied, base, copied):
    own = own_ref.shape[0]
    copied[...] = own_ref[...]
    base[...] = applied[...].astype(F32) - jnp.dot(coef[:, :own], own_ref[...], preferred_element_type=F32)


def ready(at, coef, orbitals, applied, q0, size, ratio):
    own, grid = orbitals.shape
    count = grid // size
    plane = pl.BlockSpec((own, size), lambda i, at: (0, lax.rem((at[0] - 1) * ratio + q0 + count, count)))
    return call(
        ready_body,
        (1,),
        [pl.BlockSpec(coef.shape, lambda i, at: (0, 0)), plane, plane],
        [pl.BlockSpec(memory_space=pltpu.VMEM)] * 2,
        [pltpu.VMEM((own, size), F32), pltpu.VMEM((own, size), BF16)],
        (at, coef, orbitals, applied),
    )


def finish_body(n, size, count, q0, ratio, at, coef, base, copied, sums, gram, *refs):
    rems, (_, out, margin, rows, block, others, sems) = refs[: n - 1], refs[n - 1 :]
    own = copied.shape[0]
    if n == 2:
        other = rems[0][...]
    else:
        for j in range(n - 1):
            others[j * own : (j + 1) * own, :] = rems[j][...]
        other = others[...]
    rows[:, :own] = sums[own:, :]
    rows[:, own:] = gram[...] + rowdot(copied[...], other)
    rows[...] = pltpu.roll(rows[...], at[1] * own, 1)
    first = pltpu.make_async_copy(rows, margin, sems.at[0])
    first.start()
    mixed = jnp.dot(coef[:, own:], other, preferred_element_type=F32)
    block[...] = (base[...] - mixed).astype(BF16)
    column = pl.multiple_of(lax.rem((at[0] - 1) * ratio + q0 + count, count) * size, size)
    second = pltpu.make_async_copy(block, out.at[:, pl.ds(column, size)], sems.at[1])
    second.start()
    first.wait()
    second.wait()


def finish(at, coef, base, copied, sums, rems, carry, q0, size, ratio):
    out, gram = carry
    own, grid = out.shape
    n = len(rems) + 1
    vmem, free = pl.BlockSpec(memory_space=pltpu.VMEM), pl.BlockSpec(memory_space=ANY)
    held = [pltpu.with_memory_space_constraint(a, pltpu.VMEM) for a in (coef, base, copied, sums, gram, *rems)]
    return call(
        functools.partial(finish_body, n, size, grid // size, q0, ratio),
        (1,),
        [vmem] * len(held) + [free],
        [free, free],
        [jax.ShapeDtypeStruct(out.shape, BF16), jax.ShapeDtypeStruct((own, n * own), F32)],
        (at, *held, out),
        scratch=[
            pltpu.VMEM((own, n * own), F32),
            pltpu.VMEM((own, size), BF16),
            pltpu.VMEM(((n - 1) * own, size), BF16),
            pltpu.SemaphoreType.DMA((2,)),
        ],
        aliases={len(held) + 1: 0},
    )


def cuts(count):
    out = []
    while count:
        out.append(max(1, count // 2))
        count -= out[-1]
    return out


def plan(n, side):
    share = side // n
    short = max(2, share // 4)
    widths = [2] + ([share - short, short] if share >= 4 else [share])
    widths.append((side - share - 2) // 3)
    after = cuts(PARTS * (side - sum(widths)))
    early = [(sum(widths[:c]), w, 1) for c, w in enumerate(widths)]
    late = [(PARTS * sum(widths) + sum(after[:c]), w, PARTS) for c, w in enumerate(after)]
    return early, late


def shards(n, orbitals, potential):
    own, grid = orbitals.shape
    side = round(grid ** (1 / 3))
    share = side // n
    me = lax.axis_index("band")
    potential = potential.reshape(1, grid)

    def sent(c, q0, width, ratio):
        got, count = [], side * ratio
        for j in range(1, n):
            dest = lax.rem(me + n - j, n)
            start = lax.rem((dest * share - 1) * ratio + q0 + count, count).astype(jnp.int32).reshape(1)
            chunk = (pack if c else grab)(orbitals, start, width, grid // count)
            got.append(lax.ppermute(chunk, "band", [(k, (k - j) % n) for k in range(n)]))
        return got

    early, late = plan(n, side)
    at = jnp.stack([me * share, me]).astype(jnp.int32)
    chunks = [(*block, sent(c, *block)) for c, block in enumerate(early)]
    applied, sums = apply_own(orbitals, potential, at, side)
    before = None
    for c in range(1, len(early) - 1):
        q0, w, _, rems = chunks[c]
        before = part(
            orbitals, applied, potential, at, rems, chunks[c - 1][3],
            None if before is None else before[0], q0, w, c == len(early) - 2, side,
        )
    mine, others = before[0], before[1:]
    got = []
    for j in range(1, n):
        perm = [(k, (k - j) % n) for k in range(n)]
        got.append(lax.ppermute(others[j - 1][:, own:], "band", perm))
    chunks += [(*block, sent(len(early) + c, *block)) for c, block in enumerate(late)]
    projected, coef = coefficients(at[1:], sums, mine, got)
    carry = None
    q0, _, ratio, rems = chunks.pop()
    size = grid // (side * ratio)
    base, copied = ready(at, coef, orbitals, applied, q0, size, ratio)
    for first, width, parts, block in chunks:
        carry = rest(at, coef, orbitals, applied, block, carry, first, width, grid // (side * parts), parts)
    carry = finish(at, coef, base, copied, sums, rems, carry, q0, size, ratio)
    residuals, margin = carry
    return margin, projected, residuals


def solution(mesh):
    n, spec = mesh.shape["band"], P(("frag", "band"), None)

    def body(orbitals, potential):
        return shards(n, orbitals, potential)

    return jax.shard_map(
        body,
        mesh=mesh,
        in_specs=(spec, P("frag")),
        out_specs=(spec, spec, spec),
        check_vma=False,
    )
```

```python
import functools

import jax
import jax.numpy as jnp
from jax import lax
from jax.experimental import pallas as pl
from jax.experimental.pallas import tpu as pltpu
from jax.sharding import PartitionSpec as P


ROWS = 16
WHOLE = 2**20
PARTS = 2
NARROW = 2
F32 = jnp.float32
BF16 = jnp.bfloat16
ANY = pl.ANY


def call(kernel, grid, in_specs, out_specs, out_shape, args, scratch=(), aliases={}, flops=0, limit=16):
    args = [pltpu.with_memory_space_constraint(a, pltpu.HBM) if a.size >= WHOLE else a for a in args]
    touched = sum(a.size * a.dtype.itemsize for a in args)
    return pl.pallas_call(
        kernel,
        out_shape=out_shape,
        grid_spec=pltpu.PrefetchScalarGridSpec(
            num_scalar_prefetch=1, grid=grid, in_specs=in_specs, out_specs=out_specs, scratch_shapes=scratch
        ),
        input_output_aliases=aliases,
        compiler_params=pltpu.CompilerParams(
            dimension_semantics=("arbitrary",), vmem_limit_bytes=limit * 2**20
        ),
        cost_estimate=pl.CostEstimate(flops=flops, bytes_accessed=touched, transcendentals=0),
    )(*args)


def near(ctr, left, right, pot, side):
    size = side * side
    z = lax.broadcasted_iota(jnp.int32, ctr.shape, 1) % side
    low = jnp.where(z == 0, pltpu.roll(ctr, size - side + 1, 1), pltpu.roll(ctr, 1, 1))
    high = jnp.where(z == side - 1, pltpu.roll(ctr, side - 1, 1), pltpu.roll(ctr, size - 1, 1))
    beside = (left + right) + (pltpu.roll(ctr, side, 1) + pltpu.roll(ctr, size - side, 1)) + (low + high)
    return (3.0 + pot) * ctr - 0.5 * beside


def rowdot(a, b):
    return lax.dot_general(a, b, (((1,), (1,)), ((), ())), preferred_element_type=F32)


def pack_body(at, src, dst):
    dst[...] = src[...]


def pack(orbitals, start, width, size):
    own, count = orbitals.shape[0], orbitals.shape[1] // size
    return call(
        pack_body,
        (width,),
        [pl.BlockSpec((own, size), lambda i, at: (0, lax.rem(at[0] + i, count)))],
        pl.BlockSpec((own, size), lambda i, at: (0, i)),
        jax.ShapeDtypeStruct((own, width * size), BF16),
        (start, orbitals),
    )


def grab_body(width, size, count, at, src, dst, sems):
    copies = []
    for i in range(width):
        column = pl.multiple_of(lax.rem(at[0] + i, count) * size, size)
        copies.append(
            pltpu.make_async_copy(src.at[:, pl.ds(column, size)], dst.at[:, pl.ds(i * size, size)], sems.at[i])
        )
    for copy in copies:
        copy.start()
    for copy in copies:
        copy.wait()


def grab(orbitals, start, width, size):
    own, count = orbitals.shape[0], orbitals.shape[1] // size
    return call(
        functools.partial(grab_body, width, size, count),
        (1,),
        [pl.BlockSpec(memory_space=ANY)],
        pl.BlockSpec(memory_space=pltpu.VMEM),
        pltpu.VMEM((own, width * size), BF16),
        (start, orbitals),
        scratch=[pltpu.SemaphoreType.DMA((width,))],
    )


def apply_body(side, at, left, ctr, right, pot, out, sums, both):
    own = ctr.shape[0]

    def some(r, _):
        rows = pl.ds(r * ROWS, ROWS)
        value = near(
            ctr[rows, :].astype(F32), left[rows, :].astype(F32), right[rows, :].astype(F32), pot[...], side
        )
        out[rows, :] = value.astype(BF16)
        return 0

    lax.fori_loop(0, own // ROWS, some, 0)
    both[:own, :] = out[...]
    both[own:, :] = ctr[...]

    @pl.when(pl.program_id(0) == 0)
    def _():
        sums[...] = jnp.zeros_like(sums)

    sums[...] += rowdot(both[...], ctr[...])


def apply_own(orbitals, potential, token, side):
    own, grid, size = orbitals.shape[0], orbitals.shape[1], side * side

    def plane(shift):
        return pl.BlockSpec((own, size), lambda i, at: (0, lax.rem(i + shift + side, side)))

    return call(
        functools.partial(apply_body, side),
        (side,),
        [plane(-1), plane(0), plane(1), pl.BlockSpec((1, size), lambda i, at: (0, i))],
        [plane(0), pl.BlockSpec((2 * own, own), lambda i, at: (0, 0))],
        [pltpu.HBM((own, grid), BF16), jax.ShapeDtypeStruct((2 * own, own), F32)],
        (token, orbitals, orbitals, orbitals, potential),
        scratch=[pltpu.VMEM((2 * own, size), BF16)],
        flops=4 * own * own * grid,
    )


def part_body(side, n, q0, first, last, at, own_ref, applied, pot, *refs):
    refs = list(refs)
    rems, olds, recent = refs[: n - 1], refs[n - 1 : 2 * n - 2], refs[2 * n - 2 : 3 * n - 3]
    refs = refs[3 * n - 3 :]
    before = None if first else refs.pop(0)
    outs, (ring, every, moved, total) = refs[:-4], refs[-4:]
    own = own_ref.shape[0]
    i = pl.program_id(0)

    @pl.when(i == 0)
    def _():
        for j in range(n - 1):
            rows = pl.ds(j * own, own)
            ring[(q0 - 2) % 3, rows, :] = olds[j][...]
            ring[(q0 - 1) % 3, rows, :] = recent[j][...]
        total[...] = jnp.zeros_like(total) if first else before[...]

    slot = lax.rem(q0 + i, 3)
    here = lax.rem(q0 + i + 2, 3)
    back = lax.rem(q0 + i + 1, 3)
    for j in range(n - 1):
        ring[slot, pl.ds(j * own, own), :] = rems[j][...]
    every[:own, :] = own_ref[...]
    moved[:own, :] = applied[...]

    def some(r, _):
        rows = pl.ds(r * ROWS, ROWS)
        ctr = ring[here, rows, :]
        value = near(
            ctr.astype(F32), ring[back, rows, :].astype(F32), ring[slot, rows, :].astype(F32), pot[...], side
        )
        there = pl.ds(pl.multiple_of(own + r * ROWS, ROWS), ROWS)
        every[there, :] = ctr
        moved[there, :] = value.astype(BF16)
        return 0

    lax.fori_loop(0, (n - 1) * own // ROWS, some, 0)
    total[...] += rowdot(moved[...], every[...])

    @pl.when(i == pl.num_programs(0) - 1)
    def _():
        if not last:
            outs[0][...] = total[...]
        else:
            for j in range(n):
                rows = total[((n - j) % n) * own : ((n - j) % n) * own + own, :]
                outs[j][...] = pltpu.roll(rows, j * own, 1) if j else rows


def part(orbitals, applied, potential, at, rems, previous, before, q0, width, last, side):
    own, size, n = orbitals.shape[0], side * side, len(rems) + 1
    total = n * own
    held = previous[0].shape[1] // size

    def plane():
        return pl.BlockSpec((own, size), lambda i, at: (0, lax.rem(at[0] + q0 + i - 2 + side, side)))

    def fixed(shape, column=0):
        return pl.BlockSpec(shape, lambda i, at: (0, column))

    first = before is None
    args = [at, orbitals, applied, potential, *rems, *previous, *previous] + ([] if first else [before])
    specs = [plane(), plane(), pl.BlockSpec((1, size), lambda i, at: (0, lax.rem(at[0] + q0 + i - 2 + side, side)))]
    specs += [pl.BlockSpec((own, size), lambda i, at: (0, i))] * (n - 1)
    specs += [fixed((own, size), held - 2)] * (n - 1) + [fixed((own, size), held - 1)] * (n - 1)
    specs += [] if first else [fixed((total, total))]
    shapes = [(own, total)] * n if last else [(total, total)]
    return call(
        functools.partial(part_body, side, n, q0, first, last),
        (width,),
        specs,
        [fixed(s) for s in shapes],
        [jax.ShapeDtypeStruct(s, F32) for s in shapes],
        tuple(args),
        scratch=[
            pltpu.VMEM((3, (n - 1) * own, size), BF16),
            pltpu.VMEM((total, size), BF16),
            pltpu.VMEM((total, size), BF16),
            pltpu.VMEM((total, total), F32),
        ],
        flops=2 * total * total * size * width,
    )


def coef_body(n, at, sums, mine, *refs):
    got, (projected, coef, work) = refs[: n - 1], refs[n - 1 :]
    own = mine.shape[0]
    other = mine[:, own:]
    for g in got:
        other = other + g[...]
    work[:, :own] = sums[:own, :]
    work[:, own:] = other
    gram = sums[own:, :]
    same = lax.broadcasted_iota(jnp.int32, gram.shape, 0) == lax.broadcasted_iota(jnp.int32, gram.shape, 1)
    diagonal = jnp.sum(jnp.where(same, gram, 0.0), axis=1, keepdims=True)
    value = work[...]
    coef[...] = (value / diagonal).astype(BF16)
    projected[...] = pltpu.roll(value, at[0] * own, 1)


def coefficients(at, sums, mine, got):
    own, total = mine.shape
    n = total // own

    def whole(x):
        return pl.BlockSpec(x.shape, lambda i, at: (0, 0))

    shape = jax.ShapeDtypeStruct((own, total), F32)
    return call(
        functools.partial(coef_body, n),
        (1,),
        [whole(sums), whole(mine)] + [whole(g) for g in got],
        [whole(shape), whole(shape)],
        [shape, jax.ShapeDtypeStruct((own, total), BF16)],
        (at, sums, mine, *got),
        scratch=[pltpu.VMEM((own, total), F32)],
    )


def rest_body(n, first, at, coef, own_ref, applied, *refs):
    refs = list(refs)
    rems, refs = refs[: n - 1], refs[n - 1 :]
    if not first:
        before, refs = refs[1], refs[2:]
    out, gram, every = refs
    own = own_ref.shape[0]
    every[:own, :] = own_ref[...]
    for j in range(n - 1):
        every[(j + 1) * own : (j + 2) * own, :] = rems[j][...]
    mixed = jnp.dot(coef[...], every[...], preferred_element_type=F32)
    out[...] = (applied[...].astype(F32) - mixed).astype(BF16)

    @pl.when(pl.program_id(0) == 0)
    def _():
        gram[...] = jnp.zeros_like(gram) if first else before[...]

    gram[...] += rowdot(own_ref[...], every[own:, :])


def rest(at, coef, orbitals, applied, rems, carry, q0, width, size, ratio):
    own, grid, n = orbitals.shape[0], orbitals.shape[1], len(rems) + 1
    total, count = n * own, grid // size

    def plane():
        return pl.BlockSpec((own, size), lambda i, at: (0, lax.rem((at[0] - 1) * ratio + q0 + i + count, count)))

    def fixed(shape):
        return pl.BlockSpec(shape, lambda i, at: (0, 0))

    first = carry is None
    args = [at, coef, orbitals, applied, *rems]
    specs = [fixed((own, total)), plane(), plane()]
    specs += [pl.BlockSpec((own, size), lambda i, at: (0, i))] * (n - 1)
    aliases = {}
    if not first:
        aliases = {len(args): 0}
        args += list(carry)
        specs += [pl.BlockSpec(memory_space=ANY), fixed((own, total - own))]
    return call(
        functools.partial(rest_body, n, first),
        (width,),
        specs,
        [plane(), fixed((own, total - own))],
        [jax.ShapeDtypeStruct((own, grid), BF16), jax.ShapeDtypeStruct((own, total - own), F32)],
        tuple(args),
        scratch=[pltpu.VMEM((total, size), BF16)],
        aliases=aliases,
        flops=4 * own * total * size * width,
    )


def ready_body(at, coef, own_ref, applied, base, copied):
    own, size = own_ref.shape
    columns = pl.ds(pl.multiple_of(pl.program_id(0) * size, size), size)
    copied[:, columns] = own_ref[...]
    base[:, columns] = applied[...].astype(F32) - jnp.dot(coef[:, :own], own_ref[...], preferred_element_type=F32)


def ready(at, coef, orbitals, applied, q0, width, size, ratio):
    own, grid = orbitals.shape
    count = grid // size
    plane = pl.BlockSpec((own, size), lambda i, at: (0, lax.rem((at[0] - 1) * ratio + q0 + i + count, count)))
    return call(
        ready_body,
        (width,),
        [pl.BlockSpec(coef.shape, lambda i, at: (0, 0)), plane, plane],
        [pl.BlockSpec(memory_space=pltpu.VMEM)] * 2,
        [pltpu.VMEM((own, width * size), F32), pltpu.VMEM((own, width * size), BF16)],
        (at, coef, orbitals, applied),
    )


def finish_body(n, size, count, q0, width, offset, ratio, last, at, coef, base, copied, sums, gram, *refs):
    rems, (_, out, margin, rows, block, others, sems) = refs[: n - 1], refs[n - 1 :]
    own = copied.shape[0]
    here = slice(offset * size, (offset + width) * size)
    if n == 2:
        other = rems[0][...]
    else:
        for j in range(n - 1):
            others[j * own : (j + 1) * own, :] = rems[j][...]
        other = others[...]
    mixed = jnp.dot(coef[:, own:], other, preferred_element_type=F32)
    block[...] = (base[:, here] - mixed).astype(BF16)
    copies = []
    for i in range(width):
        column = pl.multiple_of(lax.rem((at[0] - 1) * ratio + q0 + i + count, count) * size, size)
        copies.append(
            pltpu.make_async_copy(
                block.at[:, pl.ds(i * size, size)], out.at[:, pl.ds(column, size)], sems.at[i]
            )
        )
        copies[-1].start()
    total = gram[...] + rowdot(copied[:, here], other)
    if last:
        rows[:, :own] = sums[own:, :]
        rows[:, own:] = total
        rows[...] = pltpu.roll(rows[...], at[1] * own, 1)
        copies.append(pltpu.make_async_copy(rows, margin, sems.at[width]))
        copies[-1].start()
    else:
        margin[...] = total
    for copy in copies:
        copy.wait()


def finish(at, coef, base, copied, sums, rems, carry, q0, width, offset, size, ratio, last):
    out, gram = carry
    own, grid = out.shape
    n = len(rems) + 1
    vmem, free = pl.BlockSpec(memory_space=pltpu.VMEM), pl.BlockSpec(memory_space=ANY)
    held = [pltpu.with_memory_space_constraint(a, pltpu.VMEM) for a in (coef, base, copied, sums, gram, *rems)]
    return call(
        functools.partial(finish_body, n, size, grid // size, q0, width, offset, ratio, last),
        (1,),
        [vmem] * len(held) + [free],
        [free, free if last else vmem],
        [
            jax.ShapeDtypeStruct(out.shape, BF16),
            jax.ShapeDtypeStruct((own, n * own), F32) if last else pltpu.VMEM(gram.shape, F32),
        ],
        (at, *held, out),
        scratch=[
            pltpu.VMEM((own, n * own), F32),
            pltpu.VMEM((own, width * size), BF16),
            pltpu.VMEM(((n - 1) * own, width * size), BF16),
            pltpu.SemaphoreType.DMA((width + 1,)),
        ],
        aliases={len(held) + 1: 0},
    )


def cuts(count):
    out = []
    while count:
        out.append(max(1, count // 2))
        count -= out[-1]
    return out


def plan(n, side):
    share = side // n
    short = max(2, share // 4)
    widths = [2] + ([share - short, short] if share >= 4 else [share])
    widths.append((side - share - 2) // 3)
    after = cuts(PARTS * (side - sum(widths)))
    early = [(sum(widths[:c]), w, 1) for c, w in enumerate(widths)]
    late = [(PARTS * sum(widths) + sum(after[:c]), w, PARTS) for c, w in enumerate(after)]
    return early, late


def shards(n, orbitals, potential):
    own, grid = orbitals.shape
    side = round(grid ** (1 / 3))
    share = side // n
    me = lax.axis_index("band")
    potential = potential.reshape(1, grid)

    def sent(c, q0, width, ratio):
        got, count = [], side * ratio
        for j in range(1, n):
            dest = lax.rem(me + n - j, n)
            start = lax.rem((dest * share - 1) * ratio + q0 + count, count).astype(jnp.int32).reshape(1)
            chunk = (pack if c else grab)(orbitals, start, width, grid // count)
            got.append(lax.ppermute(chunk, "band", [(k, (k - j) % n) for k in range(n)]))
        return got

    early, late = plan(n, side)
    at = jnp.stack([me * share, me]).astype(jnp.int32)
    chunks = [(*block, sent(c, *block)) for c, block in enumerate(early)]
    applied, sums = apply_own(orbitals, potential, at, side)
    before = None
    for c in range(1, len(early) - 1):
        q0, w, _, rems = chunks[c]
        before = part(
            orbitals, applied, potential, at, rems, chunks[c - 1][3],
            None if before is None else before[0], q0, w, c == len(early) - 2, side,
        )
    mine, others = before[0], before[1:]
    got = []
    for j in range(1, n):
        perm = [(k, (k - j) % n) for k in range(n)]
        got.append(lax.ppermute(others[j - 1][:, own:], "band", perm))
    chunks += [(*block, sent(len(early) + c, *block)) for c, block in enumerate(late)]
    projected, coef = coefficients(at[1:], sums, mine, got)
    narrow = [chunk for chunk in chunks if chunk[2] == PARTS and chunk[1] <= NARROW]
    size, low = grid // (side * PARTS), narrow[0][0]
    base, copied = ready(at, coef, orbitals, applied, low, side * PARTS - low, size, PARTS)
    carry = None
    for q0, width, ratio, rems in chunks[: -len(narrow)]:
        carry = rest(at, coef, orbitals, applied, rems, carry, q0, width, grid // (side * ratio), ratio)
    for q0, width, _, rems in narrow:
        last = q0 + width == side * PARTS
        carry = finish(at, coef, base, copied, sums, rems, carry, q0, width, q0 - low, size, PARTS, last)
    residuals, margin = carry
    return margin, projected, residuals


def solution(mesh):
    n, spec = mesh.shape["band"], P(("frag", "band"), None)

    def body(orbitals, potential):
        return shards(n, orbitals, potential)

    return jax.shard_map(
        body,
        mesh=mesh,
        in_specs=(spec, P("frag")),
        out_specs=(spec, spec, spec),
        check_vma=False,
    )
```

```python
import functools

import jax
import jax.numpy as jnp
from jax import lax
from jax.experimental import pallas as pl
from jax.experimental.pallas import tpu as pltpu
from jax.sharding import PartitionSpec as P


ROWS = 16
WHOLE = 2**20
PARTS = 2
NARROW = 2
F32 = jnp.float32
BF16 = jnp.bfloat16
ANY = pl.ANY


def call(kernel, grid, in_specs, out_specs, out_shape, args, scratch=(), aliases={}, flops=0, limit=16, scalars=1):
    args = [pltpu.with_memory_space_constraint(a, pltpu.HBM) if a.size >= WHOLE else a for a in args]
    touched = sum(a.size * a.dtype.itemsize for a in args)
    return pl.pallas_call(
        kernel,
        out_shape=out_shape,
        grid_spec=pltpu.PrefetchScalarGridSpec(
            num_scalar_prefetch=scalars, grid=grid, in_specs=in_specs, out_specs=out_specs, scratch_shapes=scratch
        ),
        input_output_aliases=aliases,
        compiler_params=pltpu.CompilerParams(
            dimension_semantics=("arbitrary",), vmem_limit_bytes=limit * 2**20
        ),
        cost_estimate=pl.CostEstimate(flops=flops, bytes_accessed=touched, transcendentals=0),
    )(*args)


def near(ctr, left, right, pot, side):
    size = side * side
    z = lax.broadcasted_iota(jnp.int32, ctr.shape, 1) % side
    low = jnp.where(z == 0, pltpu.roll(ctr, size - side + 1, 1), pltpu.roll(ctr, 1, 1))
    high = jnp.where(z == side - 1, pltpu.roll(ctr, side - 1, 1), pltpu.roll(ctr, size - 1, 1))
    beside = (left + right) + (pltpu.roll(ctr, side, 1) + pltpu.roll(ctr, size - side, 1)) + (low + high)
    return (3.0 + pot) * ctr - 0.5 * beside


def rowdot(a, b):
    return lax.dot_general(a, b, (((1,), (1,)), ((), ())), preferred_element_type=F32)


def pack_body(start, width, size, count, src, dst, sems):
    first, copies = start(lax.axis_index("band")), []
    for i in range(width):
        column = pl.multiple_of(lax.rem(first + i, count) * size, size)
        copies.append(
            pltpu.make_async_copy(src.at[:, pl.ds(column, size)], dst.at[:, pl.ds(i * size, size)], sems.at[i])
        )
    for copy in copies:
        copy.start()
    for copy in copies:
        copy.wait()


def pack(orbitals, start, width, size):
    own, count = orbitals.shape[0], orbitals.shape[1] // size
    return call(
        functools.partial(pack_body, start, width, size, count),
        (1,),
        [pl.BlockSpec(memory_space=ANY)],
        pl.BlockSpec(memory_space=pltpu.VMEM),
        pltpu.VMEM((own, width * size), BF16),
        (orbitals,),
        scratch=[pltpu.SemaphoreType.DMA((width,))],
        scalars=0,
    )


def apply_body(side, at, left, ctr, right, pot, out, sums, both):
    own = ctr.shape[0]

    def some(r, _):
        rows = pl.ds(r * ROWS, ROWS)
        value = near(
            ctr[rows, :].astype(F32), left[rows, :].astype(F32), right[rows, :].astype(F32), pot[...], side
        )
        out[rows, :] = value.astype(BF16)
        return 0

    lax.fori_loop(0, own // ROWS, some, 0)
    both[:own, :] = out[...]
    both[own:, :] = ctr[...]

    @pl.when(pl.program_id(0) == 0)
    def _():
        sums[...] = jnp.zeros_like(sums)

    sums[...] += rowdot(both[...], ctr[...])


def apply_own(orbitals, potential, token, side):
    own, grid, size = orbitals.shape[0], orbitals.shape[1], side * side

    def plane(shift):
        return pl.BlockSpec((own, size), lambda i, at: (0, lax.rem(i + shift + side, side)))

    return call(
        functools.partial(apply_body, side),
        (side,),
        [plane(-1), plane(0), plane(1), pl.BlockSpec((1, size), lambda i, at: (0, i))],
        [plane(0), pl.BlockSpec((2 * own, own), lambda i, at: (0, 0))],
        [pltpu.HBM((own, grid), BF16), jax.ShapeDtypeStruct((2 * own, own), F32)],
        (token, orbitals, orbitals, orbitals, potential),
        scratch=[pltpu.VMEM((2 * own, size), BF16)],
        flops=4 * own * own * grid,
    )


def part_body(side, n, q0, first, last, at, own_ref, applied, pot, *refs):
    refs = list(refs)
    rems, olds, recent = refs[: n - 1], refs[n - 1 : 2 * n - 2], refs[2 * n - 2 : 3 * n - 3]
    refs = refs[3 * n - 3 :]
    before = None if first else refs.pop(0)
    outs, (ring, every, moved, total) = refs[:-4], refs[-4:]
    own = own_ref.shape[0]
    i = pl.program_id(0)

    @pl.when(i == 0)
    def _():
        for j in range(n - 1):
            rows = pl.ds(j * own, own)
            ring[(q0 - 2) % 3, rows, :] = olds[j][...]
            ring[(q0 - 1) % 3, rows, :] = recent[j][...]
        total[...] = jnp.zeros_like(total) if first else before[...]

    slot = lax.rem(q0 + i, 3)
    here = lax.rem(q0 + i + 2, 3)
    back = lax.rem(q0 + i + 1, 3)
    for j in range(n - 1):
        ring[slot, pl.ds(j * own, own), :] = rems[j][...]
    every[:own, :] = own_ref[...]
    moved[:own, :] = applied[...]

    def some(r, _):
        rows = pl.ds(r * ROWS, ROWS)
        ctr = ring[here, rows, :]
        value = near(
            ctr.astype(F32), ring[back, rows, :].astype(F32), ring[slot, rows, :].astype(F32), pot[...], side
        )
        there = pl.ds(pl.multiple_of(own + r * ROWS, ROWS), ROWS)
        every[there, :] = ctr
        moved[there, :] = value.astype(BF16)
        return 0

    lax.fori_loop(0, (n - 1) * own // ROWS, some, 0)
    total[...] += rowdot(moved[...], every[...])

    @pl.when(i == pl.num_programs(0) - 1)
    def _():
        if not last:
            outs[0][...] = total[...]
        else:
            for j in range(n):
                rows = total[((n - j) % n) * own : ((n - j) % n) * own + own, :]
                outs[j][...] = pltpu.roll(rows, j * own, 1) if j else rows


def part(orbitals, applied, potential, at, rems, previous, before, q0, width, last, side):
    own, size, n = orbitals.shape[0], side * side, len(rems) + 1
    total = n * own
    held = previous[0].shape[1] // size

    def plane():
        return pl.BlockSpec((own, size), lambda i, at: (0, lax.rem(at[0] + q0 + i - 2 + side, side)))

    def fixed(shape, column=0):
        return pl.BlockSpec(shape, lambda i, at: (0, column))

    first = before is None
    args = [at, orbitals, applied, potential, *rems, *previous, *previous] + ([] if first else [before])
    specs = [plane(), plane(), pl.BlockSpec((1, size), lambda i, at: (0, lax.rem(at[0] + q0 + i - 2 + side, side)))]
    specs += [pl.BlockSpec((own, size), lambda i, at: (0, i))] * (n - 1)
    specs += [fixed((own, size), held - 2)] * (n - 1) + [fixed((own, size), held - 1)] * (n - 1)
    specs += [] if first else [fixed((total, total))]
    shapes = [(own, total)] * n if last else [(total, total)]
    return call(
        functools.partial(part_body, side, n, q0, first, last),
        (width,),
        specs,
        [fixed(s) for s in shapes],
        [jax.ShapeDtypeStruct(s, F32) for s in shapes],
        tuple(args),
        scratch=[
            pltpu.VMEM((3, (n - 1) * own, size), BF16),
            pltpu.VMEM((total, size), BF16),
            pltpu.VMEM((total, size), BF16),
            pltpu.VMEM((total, total), F32),
        ],
        flops=2 * total * total * size * width,
    )


def coef_body(n, at, sums, mine, *refs):
    got, (projected, coef, work) = refs[: n - 1], refs[n - 1 :]
    own = mine.shape[0]
    other = mine[:, own:]
    for g in got:
        other = other + g[...]
    work[:, :own] = sums[:own, :]
    work[:, own:] = other
    gram = sums[own:, :]
    same = lax.broadcasted_iota(jnp.int32, gram.shape, 0) == lax.broadcasted_iota(jnp.int32, gram.shape, 1)
    diagonal = jnp.sum(jnp.where(same, gram, 0.0), axis=1, keepdims=True)
    value = work[...]
    coef[...] = (value / diagonal).astype(BF16)
    projected[...] = pltpu.roll(value, at[0] * own, 1)


def coefficients(at, sums, mine, got):
    own, total = mine.shape
    n = total // own

    def whole(x):
        return pl.BlockSpec(x.shape, lambda i, at: (0, 0))

    shape = jax.ShapeDtypeStruct((own, total), F32)
    return call(
        functools.partial(coef_body, n),
        (1,),
        [whole(sums), whole(mine)] + [whole(g) for g in got],
        [whole(shape), whole(shape)],
        [shape, jax.ShapeDtypeStruct((own, total), BF16)],
        (at, sums, mine, *got),
        scratch=[pltpu.VMEM((own, total), F32)],
    )


def rest_body(n, first, at, coef, own_ref, applied, *refs):
    refs = list(refs)
    rems, refs = refs[: n - 1], refs[n - 1 :]
    if not first:
        before, refs = refs[1], refs[2:]
    out, gram, every = refs
    own = own_ref.shape[0]
    every[:own, :] = own_ref[...]
    for j in range(n - 1):
        every[(j + 1) * own : (j + 2) * own, :] = rems[j][...]
    mixed = jnp.dot(coef[...], every[...], preferred_element_type=F32)
    out[...] = (applied[...].astype(F32) - mixed).astype(BF16)

    @pl.when(pl.program_id(0) == 0)
    def _():
        gram[...] = jnp.zeros_like(gram) if first else before[...]

    gram[...] += rowdot(own_ref[...], every[own:, :])


def rest(at, coef, orbitals, applied, rems, carry, q0, width, size, ratio):
    own, grid, n = orbitals.shape[0], orbitals.shape[1], len(rems) + 1
    total, count = n * own, grid // size

    def plane():
        return pl.BlockSpec((own, size), lambda i, at: (0, lax.rem((at[0] - 1) * ratio + q0 + i + count, count)))

    def fixed(shape):
        return pl.BlockSpec(shape, lambda i, at: (0, 0))

    first = carry is None
    args = [at, coef, orbitals, applied, *rems]
    specs = [fixed((own, total)), plane(), plane()]
    specs += [pl.BlockSpec((own, size), lambda i, at: (0, i))] * (n - 1)
    aliases = {}
    if not first:
        aliases = {len(args): 0}
        args += list(carry)
        specs += [pl.BlockSpec(memory_space=ANY), fixed((own, total - own))]
    return call(
        functools.partial(rest_body, n, first),
        (width,),
        specs,
        [plane(), fixed((own, total - own))],
        [jax.ShapeDtypeStruct((own, grid), BF16), jax.ShapeDtypeStruct((own, total - own), F32)],
        tuple(args),
        scratch=[pltpu.VMEM((total, size), BF16)],
        aliases=aliases,
        flops=4 * own * total * size * width,
    )


def ready_body(at, coef, own_ref, applied, base, copied):
    own, size = own_ref.shape
    columns = pl.ds(pl.multiple_of(pl.program_id(0) * size, size), size)
    copied[:, columns] = own_ref[...]
    base[:, columns] = applied[...].astype(F32) - jnp.dot(coef[:, :own], own_ref[...], preferred_element_type=F32)


def ready(at, coef, orbitals, applied, q0, width, size, ratio):
    own, grid = orbitals.shape
    count = grid // size
    plane = pl.BlockSpec((own, size), lambda i, at: (0, lax.rem((at[0] - 1) * ratio + q0 + i + count, count)))
    return call(
        ready_body,
        (width,),
        [pl.BlockSpec(coef.shape, lambda i, at: (0, 0)), plane, plane],
        [pl.BlockSpec(memory_space=pltpu.VMEM)] * 2,
        [pltpu.VMEM((own, width * size), F32), pltpu.VMEM((own, width * size), BF16)],
        (at, coef, orbitals, applied),
    )


def finish_body(n, size, count, q0, width, offset, ratio, share, last, coef, base, copied, sums, gram, *refs):
    rems, (_, out, margin, rows, block, others, sems) = refs[: n - 1], refs[n - 1 :]
    me = lax.axis_index("band")
    own = copied.shape[0]
    here = slice(offset * size, (offset + width) * size)
    if n == 2:
        other = rems[0][...]
    else:
        for j in range(n - 1):
            others[j * own : (j + 1) * own, :] = rems[j][...]
        other = others[...]
    mixed = jnp.dot(coef[:, own:], other, preferred_element_type=F32)
    block[...] = (base[:, here] - mixed).astype(BF16)
    copies = []
    for i in range(width):
        column = pl.multiple_of(lax.rem((me * share - 1) * ratio + q0 + i + count, count) * size, size)
        copies.append(
            pltpu.make_async_copy(
                block.at[:, pl.ds(i * size, size)], out.at[:, pl.ds(column, size)], sems.at[i]
            )
        )
        copies[-1].start()
    total = gram[...] + rowdot(copied[:, here], other)
    if last:
        rows[:, :own] = sums[own:, :]
        rows[:, own:] = total
        rows[...] = pltpu.roll(rows[...], me * own, 1)
        copies.append(pltpu.make_async_copy(rows, margin, sems.at[width]))
        copies[-1].start()
    else:
        margin[...] = total
    for copy in copies:
        copy.wait()


def finish(share, coef, base, copied, sums, rems, carry, q0, width, offset, size, ratio, last):
    out, gram = carry
    own, grid = out.shape
    n = len(rems) + 1
    vmem, free = pl.BlockSpec(memory_space=pltpu.VMEM), pl.BlockSpec(memory_space=ANY)
    held = [pltpu.with_memory_space_constraint(a, pltpu.VMEM) for a in (coef, base, copied, sums, gram, *rems)]
    return call(
        functools.partial(finish_body, n, size, grid // size, q0, width, offset, ratio, share, last),
        (1,),
        [vmem] * len(held) + [free],
        [free, free if last else vmem],
        [
            jax.ShapeDtypeStruct(out.shape, BF16),
            jax.ShapeDtypeStruct((own, n * own), F32) if last else pltpu.VMEM(gram.shape, F32),
        ],
        (*held, out),
        scratch=[
            pltpu.VMEM((own, n * own), F32),
            pltpu.VMEM((own, width * size), BF16),
            pltpu.VMEM(((n - 1) * own, width * size), BF16),
            pltpu.SemaphoreType.DMA((width + 1,)),
        ],
        aliases={len(held): 0},
        scalars=0,
    )


def plan(n, side):
    share = side // n
    short = max(2, share // 4)
    widths = [2] + ([share - short, short] if share >= 4 else [share])
    widths.append((side - share - 2) // 3)
    early = [(sum(widths[:c]), w, 1) for c, w in enumerate(widths)]
    done = sum(widths)
    wide = side - done - 2
    late = [(done, wide - wide // 2, 1), (side - 2 - wide // 2, wide // 2, 1)]
    narrow = [NARROW] + [1] * (2 * PARTS - NARROW)
    late += [(PARTS * (side - 2) + sum(narrow[:c]), w, PARTS) for c, w in enumerate(narrow)]
    return early, late


def shards(n, orbitals, potential):
    own, grid = orbitals.shape
    side = round(grid ** (1 / 3))
    share = side // n
    me = lax.axis_index("band")
    potential = potential.reshape(1, grid)

    def sent(q0, width, ratio):
        got, count = [], side * ratio
        for j in range(1, n):

            def start(me, j=j):
                return lax.rem((lax.rem(me + n - j, n) * share - 1) * ratio + q0 + count, count)

            chunk = pack(orbitals, start, width, grid // count)
            got.append(lax.ppermute(chunk, "band", [(k, (k - j) % n) for k in range(n)]))
        return got

    early, late = plan(n, side)
    at = jnp.stack([me * share, me]).astype(jnp.int32)
    chunks = [(*block, sent(*block)) for block in early]
    applied, sums = apply_own(orbitals, potential, at, side)
    before = None
    for c in range(1, len(early) - 1):
        q0, w, _, rems = chunks[c]
        before = part(
            orbitals, applied, potential, at, rems, chunks[c - 1][3],
            None if before is None else before[0], q0, w, c == len(early) - 2, side,
        )
    mine, others = before[0], before[1:]
    got = []
    for j in range(1, n):
        perm = [(k, (k - j) % n) for k in range(n)]
        got.append(lax.ppermute(others[j - 1][:, own:], "band", perm))
    chunks += [(*block, sent(*block)) for block in late]
    projected, coef = coefficients(at[1:], sums, mine, got)
    narrow = [chunk for chunk in chunks if chunk[2] == PARTS and chunk[1] <= NARROW]
    size, low = grid // (side * PARTS), narrow[0][0]
    base, copied = ready(at, coef, orbitals, applied, low, side * PARTS - low, size, PARTS)
    carry = None
    for q0, width, ratio, rems in chunks[: -len(narrow)]:
        carry = rest(at, coef, orbitals, applied, rems, carry, q0, width, grid // (side * ratio), ratio)
    for q0, width, _, rems in narrow:
        last = q0 + width == side * PARTS
        carry = finish(share, coef, base, copied, sums, rems, carry, q0, width, q0 - low, size, PARTS, last)
    residuals, margin = carry
    return margin, projected, residuals


def solution(mesh):
    n, spec = mesh.shape["band"], P(("frag", "band"), None)

    def body(orbitals, potential):
        return shards(n, orbitals, potential)

    return jax.shard_map(
        body,
        mesh=mesh,
        in_specs=(spec, P("frag")),
        out_specs=(spec, spec, spec),
        check_vma=False,
    )
```

```python
import functools

import jax
import jax.numpy as jnp
from jax import lax
from jax.experimental import pallas as pl
from jax.experimental.pallas import tpu as pltpu
from jax.sharding import PartitionSpec as P


ROWS = 16
WHOLE = 2**20
PARTS = 2
NARROW = 2
F32 = jnp.float32
BF16 = jnp.bfloat16
ANY = pl.ANY


def call(kernel, grid, in_specs, out_specs, out_shape, args, scratch=(), aliases={}, flops=0, limit=16, scalars=1):
    args = [pltpu.with_memory_space_constraint(a, pltpu.HBM) if a.size >= WHOLE else a for a in args]
    touched = sum(a.size * a.dtype.itemsize for a in args)
    return pl.pallas_call(
        kernel,
        out_shape=out_shape,
        grid_spec=pltpu.PrefetchScalarGridSpec(
            num_scalar_prefetch=scalars, grid=grid, in_specs=in_specs, out_specs=out_specs, scratch_shapes=scratch
        ),
        input_output_aliases=aliases,
        compiler_params=pltpu.CompilerParams(
            dimension_semantics=("arbitrary",), vmem_limit_bytes=limit * 2**20
        ),
        cost_estimate=pl.CostEstimate(flops=flops, bytes_accessed=touched, transcendentals=0),
    )(*args)


def near(ctr, left, right, pot, side):
    size = side * side
    z = lax.broadcasted_iota(jnp.int32, ctr.shape, 1) % side
    low = jnp.where(z == 0, pltpu.roll(ctr, size - side + 1, 1), pltpu.roll(ctr, 1, 1))
    high = jnp.where(z == side - 1, pltpu.roll(ctr, side - 1, 1), pltpu.roll(ctr, size - 1, 1))
    beside = (left + right) + (pltpu.roll(ctr, side, 1) + pltpu.roll(ctr, size - side, 1)) + (low + high)
    return (3.0 + pot) * ctr - 0.5 * beside


def rowdot(a, b):
    return lax.dot_general(a, b, (((1,), (1,)), ((), ())), preferred_element_type=F32)


def pack_body(start, width, size, count, src, dst, sems):
    first, copies = start(lax.axis_index("band")), []
    for i in range(width):
        column = pl.multiple_of(lax.rem(first + i, count) * size, size)
        copies.append(
            pltpu.make_async_copy(src.at[:, pl.ds(column, size)], dst.at[:, pl.ds(i * size, size)], sems.at[i])
        )
    for copy in copies:
        copy.start()
    for copy in copies:
        copy.wait()


def pack(orbitals, start, width, size):
    own, count = orbitals.shape[0], orbitals.shape[1] // size
    return call(
        functools.partial(pack_body, start, width, size, count),
        (1,),
        [pl.BlockSpec(memory_space=ANY)],
        pl.BlockSpec(memory_space=pltpu.VMEM),
        pltpu.VMEM((own, width * size), BF16),
        (orbitals,),
        scratch=[pltpu.SemaphoreType.DMA((width,))],
        scalars=0,
    )


def apply_body(side, at, left, ctr, right, pot, out, sums, both):
    own = ctr.shape[0]

    def some(r, _):
        rows = pl.ds(r * ROWS, ROWS)
        value = near(
            ctr[rows, :].astype(F32), left[rows, :].astype(F32), right[rows, :].astype(F32), pot[...], side
        )
        out[rows, :] = value.astype(BF16)
        return 0

    lax.fori_loop(0, own // ROWS, some, 0)
    both[:own, :] = out[...]
    both[own:, :] = ctr[...]

    @pl.when(pl.program_id(0) == 0)
    def _():
        sums[...] = jnp.zeros_like(sums)

    sums[...] += rowdot(both[...], ctr[...])


def apply_own(orbitals, potential, token, side):
    own, grid, size = orbitals.shape[0], orbitals.shape[1], side * side

    def plane(shift):
        return pl.BlockSpec((own, size), lambda i, at: (0, lax.rem(i + shift + side, side)))

    return call(
        functools.partial(apply_body, side),
        (side,),
        [plane(-1), plane(0), plane(1), pl.BlockSpec((1, size), lambda i, at: (0, i))],
        [plane(0), pl.BlockSpec((2 * own, own), lambda i, at: (0, 0))],
        [pltpu.HBM((own, grid), BF16), jax.ShapeDtypeStruct((2 * own, own), F32)],
        (token, orbitals, orbitals, orbitals, potential),
        scratch=[pltpu.VMEM((2 * own, size), BF16)],
        flops=4 * own * own * grid,
    )


def part_body(side, n, q0, first, last, at, own_ref, applied, pot, *refs):
    refs = list(refs)
    rems, olds, recent = refs[: n - 1], refs[n - 1 : 2 * n - 2], refs[2 * n - 2 : 3 * n - 3]
    refs = refs[3 * n - 3 :]
    before = None if first else refs.pop(0)
    outs, (ring, every, moved, total) = refs[:-4], refs[-4:]
    own = own_ref.shape[0]
    i = pl.program_id(0)

    @pl.when(i == 0)
    def _():
        for j in range(n - 1):
            rows = pl.ds(j * own, own)
            ring[(q0 - 2) % 3, rows, :] = olds[j][...]
            ring[(q0 - 1) % 3, rows, :] = recent[j][...]
        total[...] = jnp.zeros_like(total) if first else before[...]

    slot = lax.rem(q0 + i, 3)
    here = lax.rem(q0 + i + 2, 3)
    back = lax.rem(q0 + i + 1, 3)
    for j in range(n - 1):
        ring[slot, pl.ds(j * own, own), :] = rems[j][...]
    every[:own, :] = own_ref[...]
    moved[:own, :] = applied[...]

    def some(r, _):
        rows = pl.ds(r * ROWS, ROWS)
        ctr = ring[here, rows, :]
        value = near(
            ctr.astype(F32), ring[back, rows, :].astype(F32), ring[slot, rows, :].astype(F32), pot[...], side
        )
        there = pl.ds(pl.multiple_of(own + r * ROWS, ROWS), ROWS)
        every[there, :] = ctr
        moved[there, :] = value.astype(BF16)
        return 0

    lax.fori_loop(0, (n - 1) * own // ROWS, some, 0)
    total[...] += rowdot(moved[...], every[...])

    @pl.when(i == pl.num_programs(0) - 1)
    def _():
        if not last:
            outs[0][...] = total[...]
        else:
            for j in range(n):
                rows = total[((n - j) % n) * own : ((n - j) % n) * own + own, :]
                outs[j][...] = pltpu.roll(rows, j * own, 1) if j else rows


def part(orbitals, applied, potential, at, rems, previous, before, q0, width, last, side):
    own, size, n = orbitals.shape[0], side * side, len(rems) + 1
    total = n * own
    held = previous[0].shape[1] // size

    def plane():
        return pl.BlockSpec((own, size), lambda i, at: (0, lax.rem(at[0] + q0 + i - 2 + side, side)))

    def fixed(shape, column=0):
        return pl.BlockSpec(shape, lambda i, at: (0, column))

    first = before is None
    args = [at, orbitals, applied, potential, *rems, *previous, *previous] + ([] if first else [before])
    specs = [plane(), plane(), pl.BlockSpec((1, size), lambda i, at: (0, lax.rem(at[0] + q0 + i - 2 + side, side)))]
    specs += [pl.BlockSpec((own, size), lambda i, at: (0, i))] * (n - 1)
    specs += [fixed((own, size), held - 2)] * (n - 1) + [fixed((own, size), held - 1)] * (n - 1)
    specs += [] if first else [fixed((total, total))]
    shapes = [(own, total)] * n if last else [(total, total)]
    return call(
        functools.partial(part_body, side, n, q0, first, last),
        (width,),
        specs,
        [fixed(s) for s in shapes],
        [jax.ShapeDtypeStruct(s, F32) for s in shapes],
        tuple(args),
        scratch=[
            pltpu.VMEM((3, (n - 1) * own, size), BF16),
            pltpu.VMEM((total, size), BF16),
            pltpu.VMEM((total, size), BF16),
            pltpu.VMEM((total, total), F32),
        ],
        flops=2 * total * total * size * width,
    )


def coef_body(n, at, sums, mine, *refs):
    got, (projected, coef, work) = refs[: n - 1], refs[n - 1 :]
    own = mine.shape[0]
    other = mine[:, own:]
    for g in got:
        other = other + g[...]
    work[:, :own] = sums[:own, :]
    work[:, own:] = other
    gram = sums[own:, :]
    same = lax.broadcasted_iota(jnp.int32, gram.shape, 0) == lax.broadcasted_iota(jnp.int32, gram.shape, 1)
    diagonal = jnp.sum(jnp.where(same, gram, 0.0), axis=1, keepdims=True)
    value = work[...]
    coef[...] = (value / diagonal).astype(BF16)
    projected[...] = pltpu.roll(value, at[0] * own, 1)


def coefficients(at, sums, mine, got):
    own, total = mine.shape
    n = total // own

    def whole(x):
        return pl.BlockSpec(x.shape, lambda i, at: (0, 0))

    shape = jax.ShapeDtypeStruct((own, total), F32)
    return call(
        functools.partial(coef_body, n),
        (1,),
        [whole(sums), whole(mine)] + [whole(g) for g in got],
        [whole(shape), whole(shape)],
        [shape, jax.ShapeDtypeStruct((own, total), BF16)],
        (at, sums, mine, *got),
        scratch=[pltpu.VMEM((own, total), F32)],
    )


def rest_body(n, first, width, size, count, ratio, share, q0, coef, own_ref, applied, *refs):
    refs = list(refs)
    rems, refs = refs[: n - 1], refs[n - 1 :]
    if not first:
        before, refs = refs[1], refs[2:]
    out, gram, mine, held, theirs, every, got, sent = refs
    own = own_ref.shape[0]
    me = lax.axis_index("band")

    def place(i):
        return pl.ds(pl.multiple_of(lax.rem((me * share - 1) * ratio + q0 + i + count, count) * size, size), size)

    def arriving(i):
        here = pl.ds(pl.multiple_of(i * size, size), size)
        copies = [
            pltpu.make_async_copy(own_ref.at[:, place(i)], mine.at[i], got.at[i, n - 1]),
            pltpu.make_async_copy(applied.at[:, place(i)], held.at[i], got.at[i, n]),
        ]
        for j in range(n - 1):
            rows = pl.ds(j * own, own)
            copies.append(pltpu.make_async_copy(rems[j].at[:, here], theirs.at[i, rows], got.at[i, j]))
        return copies

    def leaving(i):
        return pltpu.make_async_copy(held.at[i], out.at[:, place(i)], sent.at[i])

    def ask(i, _):
        for copy in arriving(i):
            copy.start()
        return 0

    def work(i, _):
        for copy in arriving(i):
            copy.wait()
        every[:own, :] = mine[i]
        every[own:, :] = theirs[i]
        mixed = jnp.dot(coef[...], every[...], preferred_element_type=F32)
        held[i] = (held[i].astype(F32) - mixed).astype(BF16)
        leaving(i).start()
        gram[...] += rowdot(mine[i], theirs[i])
        return 0

    def end(i, _):
        leaving(i).wait()
        return 0

    lax.fori_loop(0, width, ask, 0)
    gram[...] = jnp.zeros_like(gram) if first else before[...]
    lax.fori_loop(0, width, work, 0)
    lax.fori_loop(0, width, end, 0)


def rest(share, coef, orbitals, applied, rems, carry, q0, width, size, ratio):
    own, grid, n = orbitals.shape[0], orbitals.shape[1], len(rems) + 1
    total = n * own
    free = pl.BlockSpec(memory_space=ANY)

    def fixed(shape):
        return pl.BlockSpec(shape, lambda i: (0, 0))

    first = carry is None
    args = [coef, orbitals, applied, *rems]
    specs = [fixed((own, total))] + [free] * (n + 1)
    aliases = {}
    if not first:
        aliases = {len(args): 0}
        args += list(carry)
        specs += [free, fixed((own, total - own))]
    return call(
        functools.partial(rest_body, n, first, width, size, grid // size, ratio, share, q0),
        (1,),
        specs,
        [free, fixed((own, total - own))],
        [jax.ShapeDtypeStruct((own, grid), BF16), jax.ShapeDtypeStruct((own, total - own), F32)],
        tuple(args),
        scratch=[
            pltpu.VMEM((width, own, size), BF16),
            pltpu.VMEM((width, own, size), BF16),
            pltpu.VMEM((width, total - own, size), BF16),
            pltpu.VMEM((total, size), BF16),
            pltpu.SemaphoreType.DMA((width, n + 1)),
            pltpu.SemaphoreType.DMA((width,)),
        ],
        aliases=aliases,
        flops=4 * own * total * size * width,
        scalars=0,
    )


def ready_body(at, coef, own_ref, applied, base, copied):
    own, size = own_ref.shape
    columns = pl.ds(pl.multiple_of(pl.program_id(0) * size, size), size)
    copied[:, columns] = own_ref[...]
    base[:, columns] = applied[...].astype(F32) - jnp.dot(coef[:, :own], own_ref[...], preferred_element_type=F32)


def ready(at, coef, orbitals, applied, q0, width, size, ratio):
    own, grid = orbitals.shape
    count = grid // size
    plane = pl.BlockSpec((own, size), lambda i, at: (0, lax.rem((at[0] - 1) * ratio + q0 + i + count, count)))
    return call(
        ready_body,
        (width,),
        [pl.BlockSpec(coef.shape, lambda i, at: (0, 0)), plane, plane],
        [pl.BlockSpec(memory_space=pltpu.VMEM)] * 2,
        [pltpu.VMEM((own, width * size), F32), pltpu.VMEM((own, width * size), BF16)],
        (at, coef, orbitals, applied),
    )


def finish_body(n, size, count, q0, width, offset, ratio, share, last, coef, base, copied, sums, gram, *refs):
    rems, (_, out, margin, rows, block, others, sems) = refs[: n - 1], refs[n - 1 :]
    me = lax.axis_index("band")
    own = copied.shape[0]
    here = slice(offset * size, (offset + width) * size)
    if n == 2:
        other = rems[0][...]
    else:
        for j in range(n - 1):
            others[j * own : (j + 1) * own, :] = rems[j][...]
        other = others[...]
    mixed = jnp.dot(coef[:, own:], other, preferred_element_type=F32)
    block[...] = (base[:, here] - mixed).astype(BF16)
    copies = []
    for i in range(width):
        column = pl.multiple_of(lax.rem((me * share - 1) * ratio + q0 + i + count, count) * size, size)
        copies.append(
            pltpu.make_async_copy(
                block.at[:, pl.ds(i * size, size)], out.at[:, pl.ds(column, size)], sems.at[i]
            )
        )
        copies[-1].start()
    total = gram[...] + rowdot(copied[:, here], other)
    if last:
        rows[:, :own] = sums[own:, :]
        rows[:, own:] = total
        rows[...] = pltpu.roll(rows[...], me * own, 1)
        copies.append(pltpu.make_async_copy(rows, margin, sems.at[width]))
        copies[-1].start()
    else:
        margin[...] = total
    for copy in copies:
        copy.wait()


def finish(share, coef, base, copied, sums, rems, carry, q0, width, offset, size, ratio, last):
    out, gram = carry
    own, grid = out.shape
    n = len(rems) + 1
    vmem, free = pl.BlockSpec(memory_space=pltpu.VMEM), pl.BlockSpec(memory_space=ANY)
    held = [pltpu.with_memory_space_constraint(a, pltpu.VMEM) for a in (coef, base, copied, sums, gram, *rems)]
    return call(
        functools.partial(finish_body, n, size, grid // size, q0, width, offset, ratio, share, last),
        (1,),
        [vmem] * len(held) + [free],
        [free, free if last else vmem],
        [
            jax.ShapeDtypeStruct(out.shape, BF16),
            jax.ShapeDtypeStruct((own, n * own), F32) if last else pltpu.VMEM(gram.shape, F32),
        ],
        (*held, out),
        scratch=[
            pltpu.VMEM((own, n * own), F32),
            pltpu.VMEM((own, width * size), BF16),
            pltpu.VMEM(((n - 1) * own, width * size), BF16),
            pltpu.SemaphoreType.DMA((width + 1,)),
        ],
        aliases={len(held): 0},
        scalars=0,
    )


def plan(n, side):
    share = side // n
    short = max(2, share // 4)
    widths = [2] + ([share - short, short] if share >= 4 else [share])
    widths.append((side - share - 2) // 3)
    early = [(sum(widths[:c]), w, 1) for c, w in enumerate(widths)]
    done = sum(widths)
    wide = side - done - 2
    late = [(done, wide - wide // 2, 1), (side - 2 - wide // 2, wide // 2, 1)]
    narrow = [NARROW] + [1] * (2 * PARTS - NARROW)
    late += [(PARTS * (side - 2) + sum(narrow[:c]), w, PARTS) for c, w in enumerate(narrow)]
    return early, late


def shards(n, orbitals, potential):
    own, grid = orbitals.shape
    side = round(grid ** (1 / 3))
    share = side // n
    me = lax.axis_index("band")
    potential = potential.reshape(1, grid)

    def sent(q0, width, ratio):
        got, count = [], side * ratio
        for j in range(1, n):

            def start(me, j=j):
                return lax.rem((lax.rem(me + n - j, n) * share - 1) * ratio + q0 + count, count)

            chunk = pack(orbitals, start, width, grid // count)
            got.append(lax.ppermute(chunk, "band", [(k, (k - j) % n) for k in range(n)]))
        return got

    early, late = plan(n, side)
    at = jnp.stack([me * share, me]).astype(jnp.int32)
    chunks = [(*block, sent(*block)) for block in early]
    applied, sums = apply_own(orbitals, potential, at, side)
    before = None
    for c in range(1, len(early) - 1):
        q0, w, _, rems = chunks[c]
        before = part(
            orbitals, applied, potential, at, rems, chunks[c - 1][3],
            None if before is None else before[0], q0, w, c == len(early) - 2, side,
        )
    mine, others = before[0], before[1:]
    got = []
    for j in range(1, n):
        perm = [(k, (k - j) % n) for k in range(n)]
        got.append(lax.ppermute(others[j - 1][:, own:], "band", perm))
    chunks += [(*block, sent(*block)) for block in late]
    projected, coef = coefficients(at[1:], sums, mine, got)
    narrow = [chunk for chunk in chunks if chunk[2] == PARTS and chunk[1] <= NARROW]
    size, low = grid // (side * PARTS), narrow[0][0]
    base, copied = ready(at, coef, orbitals, applied, low, side * PARTS - low, size, PARTS)
    carry = None
    for q0, width, ratio, rems in chunks[: -len(narrow)]:
        carry = rest(share, coef, orbitals, applied, rems, carry, q0, width, grid // (side * ratio), ratio)
    for q0, width, _, rems in narrow:
        last = q0 + width == side * PARTS
        carry = finish(share, coef, base, copied, sums, rems, carry, q0, width, q0 - low, size, PARTS, last)
    residuals, margin = carry
    return margin, projected, residuals


def solution(mesh):
    n, spec = mesh.shape["band"], P(("frag", "band"), None)

    def body(orbitals, potential):
        return shards(n, orbitals, potential)

    return jax.shard_map(
        body,
        mesh=mesh,
        in_specs=(spec, P("frag")),
        out_specs=(spec, spec, spec),
        check_vma=False,
    )
```

```python
import functools

import jax
import jax.numpy as jnp
from jax import lax
from jax.experimental import pallas as pl
from jax.experimental.pallas import tpu as pltpu
from jax.sharding import PartitionSpec as P


ROWS = 16
WHOLE = 2**20
PARTS = 2
NARROW = 2
F32 = jnp.float32
BF16 = jnp.bfloat16
ANY = pl.ANY


def call(kernel, grid, in_specs, out_specs, out_shape, args, scratch=(), aliases={}, flops=0, limit=16, scalars=1):
    args = [pltpu.with_memory_space_constraint(a, pltpu.HBM) if a.size >= WHOLE else a for a in args]
    touched = sum(a.size * a.dtype.itemsize for a in args)
    return pl.pallas_call(
        kernel,
        out_shape=out_shape,
        grid_spec=pltpu.PrefetchScalarGridSpec(
            num_scalar_prefetch=scalars, grid=grid, in_specs=in_specs, out_specs=out_specs, scratch_shapes=scratch
        ),
        input_output_aliases=aliases,
        compiler_params=pltpu.CompilerParams(
            dimension_semantics=("arbitrary",), vmem_limit_bytes=limit * 2**20
        ),
        cost_estimate=pl.CostEstimate(flops=flops, bytes_accessed=touched, transcendentals=0),
    )(*args)


def near(ctr, left, right, pot, side):
    size = side * side
    z = lax.broadcasted_iota(jnp.int32, ctr.shape, 1) % side
    low = jnp.where(z == 0, pltpu.roll(ctr, size - side + 1, 1), pltpu.roll(ctr, 1, 1))
    high = jnp.where(z == side - 1, pltpu.roll(ctr, side - 1, 1), pltpu.roll(ctr, size - 1, 1))
    beside = (left + right) + (pltpu.roll(ctr, side, 1) + pltpu.roll(ctr, size - side, 1)) + (low + high)
    return (3.0 + pot) * ctr - 0.5 * beside


def rowdot(a, b):
    return lax.dot_general(a, b, (((1,), (1,)), ((), ())), preferred_element_type=F32)


def pack_body(start, width, size, count, src, dst, sems):
    first, copies = start(lax.axis_index("band")), []
    for i in range(width):
        column = pl.multiple_of(lax.rem(first + i, count) * size, size)
        copies.append(
            pltpu.make_async_copy(src.at[:, pl.ds(column, size)], dst.at[:, pl.ds(i * size, size)], sems.at[i])
        )
    for copy in copies:
        copy.start()
    for copy in copies:
        copy.wait()


def pack(orbitals, start, width, size):
    own, count = orbitals.shape[0], orbitals.shape[1] // size
    return call(
        functools.partial(pack_body, start, width, size, count),
        (1,),
        [pl.BlockSpec(memory_space=ANY)],
        pl.BlockSpec(memory_space=pltpu.VMEM),
        pltpu.VMEM((own, width * size), BF16),
        (orbitals,),
        scratch=[pltpu.SemaphoreType.DMA((width,))],
        scalars=0,
    )


def apply_body(side, at, left, ctr, right, pot, out, sums, both):
    own = ctr.shape[0]

    def some(r, _):
        rows = pl.ds(r * ROWS, ROWS)
        value = near(
            ctr[rows, :].astype(F32), left[rows, :].astype(F32), right[rows, :].astype(F32), pot[...], side
        )
        out[rows, :] = value.astype(BF16)
        return 0

    lax.fori_loop(0, own // ROWS, some, 0)
    both[:own, :] = out[...]
    both[own:, :] = ctr[...]

    @pl.when(pl.program_id(0) == 0)
    def _():
        sums[...] = jnp.zeros_like(sums)

    sums[...] += rowdot(both[...], ctr[...])


def apply_own(orbitals, potential, token, side):
    own, grid, size = orbitals.shape[0], orbitals.shape[1], side * side

    def plane(shift):
        return pl.BlockSpec((own, size), lambda i, at: (0, lax.rem(i + shift + side, side)))

    return call(
        functools.partial(apply_body, side),
        (side,),
        [plane(-1), plane(0), plane(1), pl.BlockSpec((1, size), lambda i, at: (0, i))],
        [plane(0), pl.BlockSpec((2 * own, own), lambda i, at: (0, 0))],
        [pltpu.HBM((own, grid), BF16), jax.ShapeDtypeStruct((2 * own, own), F32)],
        (token, orbitals, orbitals, orbitals, potential),
        scratch=[pltpu.VMEM((2 * own, size), BF16)],
        flops=4 * own * own * grid,
    )


def part_body(side, n, q0, first, last, at, own_ref, applied, pot, *refs):
    refs = list(refs)
    rems, olds, recent = refs[: n - 1], refs[n - 1 : 2 * n - 2], refs[2 * n - 2 : 3 * n - 3]
    refs = refs[3 * n - 3 :]
    before = None if first else refs.pop(0)
    outs, (ring, every, moved, total) = refs[:-4], refs[-4:]
    own = own_ref.shape[0]
    i = pl.program_id(0)

    @pl.when(i == 0)
    def _():
        for j in range(n - 1):
            rows = pl.ds(j * own, own)
            ring[(q0 - 2) % 3, rows, :] = olds[j][...]
            ring[(q0 - 1) % 3, rows, :] = recent[j][...]
        total[...] = jnp.zeros_like(total) if first else before[...]

    slot = lax.rem(q0 + i, 3)
    here = lax.rem(q0 + i + 2, 3)
    back = lax.rem(q0 + i + 1, 3)
    for j in range(n - 1):
        ring[slot, pl.ds(j * own, own), :] = rems[j][...]
    every[:own, :] = own_ref[...]
    moved[:own, :] = applied[...]

    def some(r, _):
        rows = pl.ds(r * ROWS, ROWS)
        ctr = ring[here, rows, :]
        value = near(
            ctr.astype(F32), ring[back, rows, :].astype(F32), ring[slot, rows, :].astype(F32), pot[...], side
        )
        there = pl.ds(pl.multiple_of(own + r * ROWS, ROWS), ROWS)
        every[there, :] = ctr
        moved[there, :] = value.astype(BF16)
        return 0

    lax.fori_loop(0, (n - 1) * own // ROWS, some, 0)
    total[...] += rowdot(moved[...], every[...])

    @pl.when(i == pl.num_programs(0) - 1)
    def _():
        if not last:
            outs[0][...] = total[...]
        else:
            for j in range(n):
                rows = total[((n - j) % n) * own : ((n - j) % n) * own + own, :]
                outs[j][...] = pltpu.roll(rows, j * own, 1) if j else rows


def part(orbitals, applied, potential, at, rems, previous, before, q0, width, last, side):
    own, size, n = orbitals.shape[0], side * side, len(rems) + 1
    total = n * own
    held = previous[0].shape[1] // size

    def plane():
        return pl.BlockSpec((own, size), lambda i, at: (0, lax.rem(at[0] + q0 + i - 2 + side, side)))

    def fixed(shape, column=0):
        return pl.BlockSpec(shape, lambda i, at: (0, column))

    first = before is None
    args = [at, orbitals, applied, potential, *rems, *previous, *previous] + ([] if first else [before])
    specs = [plane(), plane(), pl.BlockSpec((1, size), lambda i, at: (0, lax.rem(at[0] + q0 + i - 2 + side, side)))]
    specs += [pl.BlockSpec((own, size), lambda i, at: (0, i))] * (n - 1)
    specs += [fixed((own, size), held - 2)] * (n - 1) + [fixed((own, size), held - 1)] * (n - 1)
    specs += [] if first else [fixed((total, total))]
    shapes = [(own, total)] * n if last else [(total, total)]
    return call(
        functools.partial(part_body, side, n, q0, first, last),
        (width,),
        specs,
        [fixed(s) for s in shapes],
        [jax.ShapeDtypeStruct(s, F32) for s in shapes],
        tuple(args),
        scratch=[
            pltpu.VMEM((3, (n - 1) * own, size), BF16),
            pltpu.VMEM((total, size), BF16),
            pltpu.VMEM((total, size), BF16),
            pltpu.VMEM((total, total), F32),
        ],
        flops=2 * total * total * size * width,
    )


def coef_body(n, sums, mine, *refs):
    got, (projected, coef, work) = refs[: n - 1], refs[n - 1 :]
    own = mine.shape[0]
    other = mine[:, own:]
    for g in got:
        other = other + g[...]
    work[:, :own] = sums[:own, :]
    work[:, own:] = other
    gram = sums[own:, :]
    same = lax.broadcasted_iota(jnp.int32, gram.shape, 0) == lax.broadcasted_iota(jnp.int32, gram.shape, 1)
    diagonal = jnp.sum(jnp.where(same, gram, 0.0), axis=1, keepdims=True)
    value = work[...]
    coef[...] = (value / diagonal).astype(BF16)
    projected[...] = pltpu.roll(value, lax.axis_index("band") * own, 1)


def coefficients(sums, mine, got):
    own, total = mine.shape
    n = total // own

    def whole(x):
        return pl.BlockSpec(x.shape, lambda i: (0, 0))

    shape = jax.ShapeDtypeStruct((own, total), F32)
    return call(
        functools.partial(coef_body, n),
        (1,),
        [whole(sums), whole(mine)] + [whole(g) for g in got],
        [whole(shape), whole(shape)],
        [shape, jax.ShapeDtypeStruct((own, total), BF16)],
        (sums, mine, *got),
        scratch=[pltpu.VMEM((own, total), F32)],
        scalars=0,
    )


def rest_body(n, first, width, size, count, ratio, share, q0, coef, own_ref, applied, *refs):
    refs = list(refs)
    rems, refs = refs[: n - 1], refs[n - 1 :]
    if not first:
        before, refs = refs[1], refs[2:]
    out, gram, mine, held, theirs, every, got, sent = refs
    own = own_ref.shape[0]
    me = lax.axis_index("band")

    def place(i):
        return pl.ds(pl.multiple_of(lax.rem((me * share - 1) * ratio + q0 + i + count, count) * size, size), size)

    def arriving(i):
        here = pl.ds(pl.multiple_of(i * size, size), size)
        copies = [
            pltpu.make_async_copy(own_ref.at[:, place(i)], mine.at[i], got.at[i, n - 1]),
            pltpu.make_async_copy(applied.at[:, place(i)], held.at[i], got.at[i, n]),
        ]
        for j in range(n - 1):
            rows = pl.ds(j * own, own)
            copies.append(pltpu.make_async_copy(rems[j].at[:, here], theirs.at[i, rows], got.at[i, j]))
        return copies

    def leaving(i):
        return pltpu.make_async_copy(held.at[i], out.at[:, place(i)], sent.at[i])

    def ask(i, _):
        for copy in arriving(i):
            copy.start()
        return 0

    def work(i, _):
        for copy in arriving(i):
            copy.wait()
        every[:own, :] = mine[i]
        every[own:, :] = theirs[i]
        mixed = jnp.dot(coef[...], every[...], preferred_element_type=F32)
        held[i] = (held[i].astype(F32) - mixed).astype(BF16)
        leaving(i).start()
        gram[...] += rowdot(mine[i], theirs[i])
        return 0

    def end(i, _):
        leaving(i).wait()
        return 0

    lax.fori_loop(0, width, ask, 0)
    gram[...] = jnp.zeros_like(gram) if first else before[...]
    lax.fori_loop(0, width, work, 0)
    lax.fori_loop(0, width, end, 0)


def rest(share, coef, orbitals, applied, rems, carry, q0, width, size, ratio):
    own, grid, n = orbitals.shape[0], orbitals.shape[1], len(rems) + 1
    total = n * own
    free = pl.BlockSpec(memory_space=ANY)

    def fixed(shape):
        return pl.BlockSpec(shape, lambda i: (0, 0))

    first = carry is None
    args = [coef, orbitals, applied, *rems]
    specs = [fixed((own, total))] + [free] * (n + 1)
    aliases = {}
    if not first:
        aliases = {len(args): 0}
        args += list(carry)
        specs += [free, fixed((own, total - own))]
    return call(
        functools.partial(rest_body, n, first, width, size, grid // size, ratio, share, q0),
        (1,),
        specs,
        [free, fixed((own, total - own))],
        [jax.ShapeDtypeStruct((own, grid), BF16), jax.ShapeDtypeStruct((own, total - own), F32)],
        tuple(args),
        scratch=[
            pltpu.VMEM((width, own, size), BF16),
            pltpu.VMEM((width, own, size), BF16),
            pltpu.VMEM((width, total - own, size), BF16),
            pltpu.VMEM((total, size), BF16),
            pltpu.SemaphoreType.DMA((width, n + 1)),
            pltpu.SemaphoreType.DMA((width,)),
        ],
        aliases=aliases,
        flops=4 * own * total * size * width,
        scalars=0,
    )


def ready_body(q0, width, size, count, ratio, share, coef, own_ref, applied, base, copied, held, got):
    own, me = copied.shape[0], lax.axis_index("band")
    copies = []
    for i in range(width):
        place = pl.multiple_of(lax.rem((me * share - 1) * ratio + q0 + i + count, count) * size, size)
        here, there = pl.ds(i * size, size), pl.ds(place, size)
        copies.append(pltpu.make_async_copy(own_ref.at[:, there], copied.at[:, here], got.at[2 * i]))
        copies.append(pltpu.make_async_copy(applied.at[:, there], held.at[:, here], got.at[2 * i + 1]))
    for copy in copies:
        copy.start()
    for i in range(width):
        copies[2 * i].wait()
        copies[2 * i + 1].wait()
        here = slice(i * size, (i + 1) * size)
        mixed = jnp.dot(coef[:, :own], copied[:, here], preferred_element_type=F32)
        base[:, here] = held[:, here].astype(F32) - mixed


def ready(share, coef, orbitals, applied, q0, width, size, ratio):
    own, grid = orbitals.shape
    free = pl.BlockSpec(memory_space=ANY)
    return call(
        functools.partial(ready_body, q0, width, size, grid // size, ratio, share),
        (1,),
        [pl.BlockSpec(coef.shape, lambda i: (0, 0)), free, free],
        [pl.BlockSpec(memory_space=pltpu.VMEM)] * 2,
        [pltpu.VMEM((own, width * size), F32), pltpu.VMEM((own, width * size), BF16)],
        (coef, orbitals, applied),
        scratch=[pltpu.VMEM((own, width * size), BF16), pltpu.SemaphoreType.DMA((2 * width,))],
        scalars=0,
    )


def finish_body(n, size, count, q0, width, offset, ratio, share, last, coef, base, copied, sums, gram, *refs):
    rems, (_, out, margin, rows, block, others, sems) = refs[: n - 1], refs[n - 1 :]
    me = lax.axis_index("band")
    own = copied.shape[0]
    here = slice(offset * size, (offset + width) * size)
    if n == 2:
        other = rems[0][...]
    else:
        for j in range(n - 1):
            others[j * own : (j + 1) * own, :] = rems[j][...]
        other = others[...]
    mixed = jnp.dot(coef[:, own:], other, preferred_element_type=F32)
    block[...] = (base[:, here] - mixed).astype(BF16)
    copies = []
    for i in range(width):
        column = pl.multiple_of(lax.rem((me * share - 1) * ratio + q0 + i + count, count) * size, size)
        copies.append(
            pltpu.make_async_copy(
                block.at[:, pl.ds(i * size, size)], out.at[:, pl.ds(column, size)], sems.at[i]
            )
        )
        copies[-1].start()
    total = gram[...] + rowdot(copied[:, here], other)
    if last:
        rows[:, :own] = sums[own:, :]
        rows[:, own:] = total
        rows[...] = pltpu.roll(rows[...], me * own, 1)
        copies.append(pltpu.make_async_copy(rows, margin, sems.at[width]))
        copies[-1].start()
    else:
        margin[...] = total
    for copy in copies:
        copy.wait()


def finish(share, coef, base, copied, sums, rems, carry, q0, width, offset, size, ratio, last):
    out, gram = carry
    own, grid = out.shape
    n = len(rems) + 1
    vmem, free = pl.BlockSpec(memory_space=pltpu.VMEM), pl.BlockSpec(memory_space=ANY)
    held = [pltpu.with_memory_space_constraint(a, pltpu.VMEM) for a in (coef, base, copied, sums, gram, *rems)]
    return call(
        functools.partial(finish_body, n, size, grid // size, q0, width, offset, ratio, share, last),
        (1,),
        [vmem] * len(held) + [free],
        [free, free if last else vmem],
        [
            jax.ShapeDtypeStruct(out.shape, BF16),
            jax.ShapeDtypeStruct((own, n * own), F32) if last else pltpu.VMEM(gram.shape, F32),
        ],
        (*held, out),
        scratch=[
            pltpu.VMEM((own, n * own), F32),
            pltpu.VMEM((own, width * size), BF16),
            pltpu.VMEM(((n - 1) * own, width * size), BF16),
            pltpu.SemaphoreType.DMA((width + 1,)),
        ],
        aliases={len(held): 0},
        scalars=0,
    )


def plan(n, side):
    share = side // n
    short = max(2, share // 4)
    widths = [2] + ([share - short, short] if share >= 4 else [share])
    widths.append((side - share - 2) // 3)
    early = [(sum(widths[:c]), w, 1) for c, w in enumerate(widths)]
    done = sum(widths)
    wide = side - done - 2
    late = [(done, wide - wide // 2, 1), (side - 2 - wide // 2, wide // 2, 1)]
    narrow = [NARROW] + [1] * (2 * PARTS - NARROW)
    late += [(PARTS * (side - 2) + sum(narrow[:c]), w, PARTS) for c, w in enumerate(narrow)]
    return early, late


def shards(n, orbitals, potential):
    own, grid = orbitals.shape
    side = round(grid ** (1 / 3))
    share = side // n
    me = lax.axis_index("band")
    potential = potential.reshape(1, grid)

    def sent(q0, width, ratio):
        got, count = [], side * ratio
        for j in range(1, n):

            def start(me, j=j):
                return lax.rem((lax.rem(me + n - j, n) * share - 1) * ratio + q0 + count, count)

            chunk = pack(orbitals, start, width, grid // count)
            got.append(lax.ppermute(chunk, "band", [(k, (k - j) % n) for k in range(n)]))
        return got

    early, late = plan(n, side)
    at = jnp.stack([me * share, me]).astype(jnp.int32)
    chunks = [(*block, sent(*block)) for block in early]
    applied, sums = apply_own(orbitals, potential, at, side)
    before = None
    for c in range(1, len(early) - 1):
        q0, w, _, rems = chunks[c]
        before = part(
            orbitals, applied, potential, at, rems, chunks[c - 1][3],
            None if before is None else before[0], q0, w, c == len(early) - 2, side,
        )
    mine, others = before[0], before[1:]
    got = []
    for j in range(1, n):
        perm = [(k, (k - j) % n) for k in range(n)]
        got.append(lax.ppermute(others[j - 1][:, own:], "band", perm))
    chunks += [(*block, sent(*block)) for block in late]
    projected, coef = coefficients(sums, mine, got)
    narrow = [chunk for chunk in chunks if chunk[2] == PARTS and chunk[1] <= NARROW]
    size, low = grid // (side * PARTS), narrow[0][0]
    base, copied = ready(share, coef, orbitals, applied, low, side * PARTS - low, size, PARTS)
    carry = None
    for q0, width, ratio, rems in chunks[: -len(narrow)]:
        carry = rest(share, coef, orbitals, applied, rems, carry, q0, width, grid // (side * ratio), ratio)
    for q0, width, _, rems in narrow:
        last = q0 + width == side * PARTS
        carry = finish(share, coef, base, copied, sums, rems, carry, q0, width, q0 - low, size, PARTS, last)
    residuals, margin = carry
    return margin, projected, residuals


def solution(mesh):
    n, spec = mesh.shape["band"], P(("frag", "band"), None)

    def body(orbitals, potential):
        return shards(n, orbitals, potential)

    return jax.shard_map(
        body,
        mesh=mesh,
        in_specs=(spec, P("frag")),
        out_specs=(spec, spec, spec),
        check_vma=False,
    )
```
